256 devices in a mesh: frame: 16 (over x_lo, y, core), head: 16 (over x_hi, z).
Axes of the slice: x: 4 (x_hi: 2, x_lo: 2; x = x_hi * 2 + x_lo), y: 4, z: 8, core: 2. Of those that a mesh axis runs over, the one named last changes fastest.
Arguments:
- query_states: bfloat16 [8192, 4096], P('frame', 'head'), may hold values from -4.6 to 4.6
- key_states: bfloat16 [8192, 4096], P('frame', 'head'), may hold values from -4.6 to 4.6
- value_states: bfloat16 [8192, 4096], P('frame', 'head'), may hold values from -24 to 24
- out_weight: bfloat16 [4096, 5120], P('head'), may hold values from -0.1875 to 0.1875
- upstream: bfloat16 [8192, 5120], P('frame'), may hold values from -72 to 72
- tile_mask: int32 [32, 5], replicated, may hold values from 0 to 1, as said below
Outputs:
- attended: bfloat16 [8192, 4096], P('frame', 'head')
- projected: bfloat16 [8192, 5120], P('frame', 'head')
- grad_query: bfloat16 [8192, 4096], P('frame', 'head')
- grad_key: bfloat16 [8192, 4096], P('frame', 'head')
- grad_value: bfloat16 [8192, 4096], P('frame', 'head')
- gram_left: float32 [32, 16, 128, 128], P('head', 'frame')
- gram_right: float32 [32, 16, 320, 320], P('head', 'frame')
The draws below stay inside these ranges and needn't reach their ends.
Inputs may be any that keep to these rules, and one draw needn't show every extreme that they name: `tile_mask`: in every row, column 2 (the query tile's own tile) is 1.
All inputs are finite; a program needn't handle non-finite values.
Results may differ from the reference program's by a relative error of at most 0.019.
Values may be sent and summed in bfloat16 or wider, within the bound.
No kernel may reach another device: no remote copies, remote signals or barrier semaphores. Data moves between devices by JAX's collectives and lax.ppermute only.
A program may use at most 128 MiB of HBM per device.

```python
import math
import jax
import jax.numpy as jnp
from jax import lax

D = 5120
HD = 128
HEAD_DEV = 2
TILE = 256
TILES_DEV = 2
CB = 320
HEADS = 32
TOK_DEV = 512
TOKENS = 8192
NT = 32
WIN = 5
NB = 16
N_FRAME = 16
N_HEAD = 16


def drawn_pair(key):
    folded = jax.random.fold_in(key, 71)
    shape = (TOKENS, HEADS * HD)
    query_part = jnp.clip(jax.random.normal(jax.random.fold_in(folded, 1), shape, jnp.float32), -4.5, 4.5)
    key_part = jnp.clip(jax.random.normal(jax.random.fold_in(folded, 2), shape, jnp.float32), -4.5, 4.5)
    return (query_part, key_part)


def draw_query_states(key, part):
    return drawn_pair(key)[0].astype(jnp.bfloat16)


def draw_key_states(key, part):
    return drawn_pair(key)[1].astype(jnp.bfloat16)


def draw_upstream(key, part):
    row_index = jnp.arange(TOKENS, dtype=jnp.float32)
    rising = 1.0 + 2.0 * row_index / max(TOKENS - 1, 1)
    row_scale = rising * jnp.exp(jax.random.uniform(jax.random.fold_in(key, 11), (TOKENS,), jnp.float32, 0.0, math.log(3.0)))
    col_scale = 0.2 * jnp.exp(jax.random.uniform(jax.random.fold_in(key, 12), (D,), jnp.float32, 0.0, math.log(10.0)))
    values_drawn = jnp.clip(jax.random.normal(jax.random.fold_in(key, 13), (TOKENS, D), jnp.float32), -4.0, 4.0)
    return (values_drawn * row_scale[:, None] * col_scale[None, :]).astype(jnp.bfloat16)


def draw_tile_mask(key, part):
    random_bits = jax.random.randint(jax.random.fold_in(key, 21), (NT, WIN), 0, 2, dtype=jnp.int32)
    columns = jnp.arange(WIN, dtype=jnp.int32)[None, :]
    return jnp.where(columns == TILES_DEV, 1, random_bits).astype(jnp.int32)


def shard_levels(key, extent, split, least, largest):
    def one(position, shards_of):
        heights = jax.random.uniform(jax.random.fold_in(jax.random.fold_in(key, 6), position), (shards_of,), jnp.float32, least / len(split), largest / len(split))
        return jnp.repeat(jnp.exp(heights), extent[position] // shards_of).reshape((-1,) + (1,) * (len(extent) - position - 1))

    level = one(*split[0])
    for cut in split[1:]:
        level = level * one(*cut)
    return level


def normal_values(own_key, dims, deviation, bound, cuts=(), held_as=jnp.bfloat16):
    factor_of = shard_levels(own_key, dims, cuts, -0.22, 0.18) if cuts else 1.0
    entries = jax.random.normal(own_key, dims, jnp.float32) * deviation * factor_of
    return jnp.minimum(jnp.maximum(entries, -bound), bound).astype(held_as)


def setup_inputs(seed: int = 0) -> dict:
    splits = jax.random.split(jax.random.key(seed), 7)
    return {
        "query_states": draw_query_states(jax.random.fold_in(splits[6], 71), 0),
        "key_states": draw_key_states(jax.random.fold_in(splits[6], 71), 0),
        "value_states": normal_values(splits[2], (TOKENS, HEADS * HD), 4.0, 24.0, ((0, 16), (1, 16))),
        "out_weight": normal_values(splits[3], (HEADS * HD, D), (HEAD_DEV * HD * 4) ** -0.5, 0.1875, ((0, 16),)),
        "upstream": draw_upstream(jax.random.fold_in(splits[6], 71), 0),
        "tile_mask": draw_tile_mask(jax.random.fold_in(splits[6], 71), 0),
    }


epsilon = 1e-06

def tile_allowed(tile_mask, query_tiles, key_tiles):
    tile_count = tile_mask.shape[0]
    window = tile_mask.shape[1]
    reach_tiles = (window - 1) // 2
    row_hits = (query_tiles[:, None] == jnp.arange(tile_count, dtype=jnp.int32)[None, :]).astype(jnp.int32)
    picked = lax.optimization_barrier(jnp.sum(row_hits[:, :, None] * tile_mask[None, :, :], axis=1))
    offsets = key_tiles[None, :] - query_tiles[:, None] + reach_tiles
    col_hits = offsets[:, :, None] == jnp.arange(window, dtype=jnp.int32)[None, None, :]
    chosen = lax.optimization_barrier(jnp.sum(jnp.where(col_hits, picked[:, None, :], 0), axis=2))
    query_inside = (query_tiles >= 0) & (query_tiles < tile_count)
    key_inside = (key_tiles >= 0) & (key_tiles < tile_count)
    return (chosen > 0) & query_inside[:, None] & key_inside[None, :]

def masked_scores(queries, key_rows, query_tile, key_tile, tile_mask):
    scaling = 1.0 / math.sqrt(queries.shape[2])
    scores = jnp.einsum('thd,shd->hts', queries.astype(jnp.float32), key_rows.astype(jnp.float32)) * scaling
    heads_here = scores.shape[0]
    query_count = queries.shape[0] // TILE
    key_count = key_rows.shape[0] // TILE
    allowed = tile_allowed(tile_mask, query_tile + jnp.arange(query_count, dtype=jnp.int32), key_tile + jnp.arange(key_count, dtype=jnp.int32))
    blocked = scores.reshape(heads_here, query_count, TILE, key_count, TILE)
    blocked = jnp.where(allowed[None, :, None, :, None], blocked, jnp.float32(-1e+30))
    return blocked.reshape(scores.shape)

def log_total(scores):
    peak = lax.optimization_barrier(jnp.max(scores, axis=2))
    return peak + jnp.log(lax.optimization_barrier(jnp.sum(jnp.exp(scores - peak[:, :, None]), axis=2)))

def reference(query_states, key_states, value_states, out_weight, upstream, tile_mask):
    scaling = 1.0 / math.sqrt(HD)
    queries = query_states.reshape(TOKENS, HEADS, HD)
    key_all = key_states.reshape(TOKENS, HEADS, HD)
    value_all = value_states.reshape(TOKENS, HEADS, HD)
    padding = jnp.zeros((TOK_DEV, HEADS, HD), jnp.bfloat16)
    keys_pad = jnp.concatenate([padding, key_all, padding], axis=0)
    values_pad = jnp.concatenate([padding, value_all, padding], axis=0)
    block_ids = jnp.arange(N_FRAME, dtype=jnp.int32)

    def forward_block(block_id):
        first_row = (block_id * TOK_DEV).astype(jnp.int32)
        query_rows = lax.dynamic_slice_in_dim(queries, first_row, TOK_DEV, 0)
        key_rows = lax.dynamic_slice_in_dim(keys_pad, first_row, 3 * TOK_DEV, 0)
        value_rows = lax.dynamic_slice_in_dim(values_pad, first_row, 3 * TOK_DEV, 0)
        scores = masked_scores(query_rows, key_rows, block_id * TILES_DEV, block_id * TILES_DEV - TILES_DEV, tile_mask)
        totals = log_total(scores)
        weights = jnp.exp(scores - totals[:, :, None]).astype(jnp.bfloat16)
        output = jnp.einsum('hts,shd->thd', weights.astype(jnp.float32), value_rows.astype(jnp.float32))
        return (output.astype(jnp.bfloat16), totals)
    outputs, totals_blocks = lax.map(forward_block, block_ids)
    attended3 = outputs.reshape(TOKENS, HEADS, HD)
    attended = attended3.reshape(TOKENS, HEADS * HD)
    totals_all = jnp.transpose(totals_blocks, (1, 0, 2)).reshape(HEADS, TOKENS)
    group_width = HEAD_DEV * HD

    def add_group(group_id, running):
        first_col = (group_id * group_width).astype(jnp.int32)
        group_cols = lax.dynamic_slice_in_dim(attended, first_col, group_width, 1)
        group_rows = lax.dynamic_slice_in_dim(out_weight, first_col, group_width, 0)
        group_sum = jnp.dot(group_cols, group_rows, preferred_element_type=jnp.float32).astype(jnp.bfloat16)
        group_sum = lax.optimization_barrier(group_sum)
        return running + group_sum.astype(jnp.float32)
    projected = lax.fori_loop(0, N_HEAD, add_group, jnp.zeros((TOKENS, D), jnp.float32)).astype(jnp.bfloat16)
    grad_attended = lax.dot_general(upstream, out_weight, (((1,), (1,)), ((), ())), preferred_element_type=jnp.float32).astype(jnp.bfloat16)
    grads3 = grad_attended.reshape(TOKENS, HEADS, HD)
    deltas = lax.optimization_barrier(jnp.sum(grads3.astype(jnp.float32) * attended3.astype(jnp.float32), axis=2)).T

    def query_block(block_id):
        first_row = (block_id * TOK_DEV).astype(jnp.int32)
        query_rows = lax.dynamic_slice_in_dim(queries, first_row, TOK_DEV, 0)
        grad_rows = lax.dynamic_slice_in_dim(grads3, first_row, TOK_DEV, 0)
        key_rows = lax.dynamic_slice_in_dim(keys_pad, first_row, 3 * TOK_DEV, 0)
        value_rows = lax.dynamic_slice_in_dim(values_pad, first_row, 3 * TOK_DEV, 0)
        total_rows = lax.dynamic_slice_in_dim(totals_all, first_row, TOK_DEV, 1)
        delta_rows = lax.dynamic_slice_in_dim(deltas, first_row, TOK_DEV, 1)
        scores = masked_scores(query_rows, key_rows, block_id * TILES_DEV, block_id * TILES_DEV - TILES_DEV, tile_mask)
        attention = jnp.exp(scores - total_rows[:, :, None])
        grad_probs = jnp.einsum('thd,shd->hts', grad_rows.astype(jnp.float32), value_rows.astype(jnp.float32))
        grad_scores = (attention * (grad_probs - delta_rows[:, :, None])).astype(jnp.bfloat16)
        result = jnp.einsum('hts,shd->thd', grad_scores.astype(jnp.float32), key_rows.astype(jnp.float32)) * scaling
        return result.astype(jnp.bfloat16)
    grad_query = lax.map(query_block, block_ids).reshape(TOKENS, HEADS * HD)
    queries_pad = jnp.concatenate([padding, queries, padding], axis=0)
    grads_pad = jnp.concatenate([padding, grads3, padding], axis=0)
    stat_pad = jnp.zeros((HEADS, TOK_DEV), jnp.float32)
    totals_pad = jnp.concatenate([stat_pad, totals_all, stat_pad], axis=1)
    deltas_pad = jnp.concatenate([stat_pad, deltas, stat_pad], axis=1)

    def key_block(block_id):
        first_row = (block_id * TOK_DEV).astype(jnp.int32)
        query_rows = lax.dynamic_slice_in_dim(queries_pad, first_row, 3 * TOK_DEV, 0)
        grad_rows = lax.dynamic_slice_in_dim(grads_pad, first_row, 3 * TOK_DEV, 0)
        total_rows = lax.dynamic_slice_in_dim(totals_pad, first_row, 3 * TOK_DEV, 1)
        delta_rows = lax.dynamic_slice_in_dim(deltas_pad, first_row, 3 * TOK_DEV, 1)
        key_rows = lax.dynamic_slice_in_dim(key_all, first_row, TOK_DEV, 0)
        value_rows = lax.dynamic_slice_in_dim(value_all, first_row, TOK_DEV, 0)
        scores = masked_scores(query_rows, key_rows, block_id * TILES_DEV - TILES_DEV, block_id * TILES_DEV, tile_mask)
        attention = jnp.exp(scores - total_rows[:, :, None])
        weights = attention.astype(jnp.bfloat16)
        grad_probs = jnp.einsum('thd,shd->hts', grad_rows.astype(jnp.float32), value_rows.astype(jnp.float32))
        grad_scores = (attention * (grad_probs - delta_rows[:, :, None])).astype(jnp.bfloat16)
        grad_keys = jnp.einsum('hts,thd->shd', grad_scores.astype(jnp.float32), query_rows.astype(jnp.float32)) * scaling
        grad_values = jnp.einsum('hts,thd->shd', weights.astype(jnp.float32), grad_rows.astype(jnp.float32))
        return (grad_keys.astype(jnp.bfloat16), grad_values.astype(jnp.bfloat16))
    grad_keys, grad_values = lax.map(key_block, block_ids)
    grad_key = grad_keys.reshape(TOKENS, HEADS * HD)
    grad_value = grad_values.reshape(TOKENS, HEADS * HD)
    weight_grad = lax.dot_general(attended, upstream, (((0,), (0,)), ((), ())), preferred_element_type=jnp.float32)
    blocks = weight_grad.reshape(HEADS, HD, NB, CB)
    highest = lax.Precision.HIGHEST
    traces = jnp.einsum('hebc,hebc->hb', blocks, blocks, precision=highest)
    divisor = (traces + epsilon)[:, :, None, None]
    gram_left = HD * jnp.einsum('hebc,hfbc->hbef', blocks, blocks, precision=highest) / divisor
    gram_right = CB * jnp.einsum('hebc,hebd->hbcd', blocks, blocks, precision=highest) / divisor
    return (attended, projected, grad_query, grad_key, grad_value, gram_left, gram_right)
```

```python
import math

import jax
import jax.numpy as jnp
from jax import lax
from jax.experimental import pallas as pl
from jax.experimental.pallas import tpu as pltpu
from jax.sharding import Mesh
from jax.sharding import PartitionSpec as P


D = 5120
HD = 128
TILE = 256
TILES_DEV = 2
CB = 320
TOK = 512
NT = 32
WIN = 5
GROUP = 2 * CB
GROUPS = D // GROUP
FRAME = ("xlo", "y", "core")
HEAD = ("xhi", "zq", "zp")
NEAR = ("xhi", "zp")

epsilon = 1e-06
SCALING = 1.0 / math.sqrt(HD)
LOG2E = 1.0 / math.log(2.0)
NEG = -1e30
VMEM_BYTES = 16 * 1024 * 1024
PLANE = 8


def dot_nt(a, b, precision=None):
    return lax.dot_general(
        a, b, (((1,), (1,)), ((), ())), precision=precision, preferred_element_type=jnp.float32
    )


def dot_nn(a, b):
    return jnp.dot(a, b, preferred_element_type=jnp.float32)


def eye(n):
    rows = lax.broadcasted_iota(jnp.int32, (n, n), 0)
    cols = lax.broadcasted_iota(jnp.int32, (n, n), 1)
    return (rows == cols).astype(jnp.float32).astype(jnp.bfloat16)


def allowed(ids, mask, i, j):
    tile = ids[0] * TILES_DEV + i
    key_tile = tile + (j - 2)
    return (mask[j, tile] == 1) & (key_tile >= 0) & (key_tile < NT)


def extend(pieces, target):
    for place, piece in enumerate(pieces):
        target[place * TOK : (place + 1) * TOK] = piece[...]


def forward_kernel(ids, mask, q, kl, k, kr, vl, v, vr, att, copy, stat, kx, vx):
    extend((kl, k, kr), kx)
    extend((vl, v, vr), vx)
    first_lane = lax.broadcasted_iota(jnp.int32, (8, HD), 1) == 0
    pick = jnp.where(first_lane, jnp.float32(1), jnp.float32(0))
    for i in range(TILES_DEV):
        rows = slice(i * TILE, (i + 1) * TILE)
        parts = []
        for j in range(WIN):
            keys = kx[(i + j) * TILE : (i + j + 1) * TILE]
            part = dot_nt(q[rows], keys) * jnp.float32(SCALING * LOG2E)
            parts.append(jnp.where(allowed(ids, mask, i, j), part, jnp.float32(NEG)))
        peak = parts[0]
        for part in parts[1:]:
            peak = jnp.maximum(peak, part)
        peak = jnp.max(peak, axis=1, keepdims=True)
        out = jnp.zeros((TILE, HD), jnp.float32)
        total = jnp.zeros((TILE, TILE), jnp.float32)
        for j in range(WIN):
            weight = jnp.exp2(parts[j] - peak)
            total = total + weight
            values = vx[(i + j) * TILE : (i + j + 1) * TILE]
            out = out + dot_nn(weight.astype(jnp.bfloat16), values)
        total = jnp.sum(total, axis=1, keepdims=True)
        att[rows] = (out / total).astype(jnp.bfloat16)
        copy[rows] = att[rows]
        log_total = peak + jnp.log(total) * jnp.float32(LOG2E)
        spread = jnp.broadcast_to(log_total, (TILE, HD))
        stat[0, :, rows] = dot_nt(pick, spread, lax.Precision.HIGHEST)


def backward_kernel(
    ids, mask, q, kl, k, kr, vl, v, vr, g, att, stat, dq, dl, do, dr, kx, vx, dsx, kt
):
    extend((kl, k, kr), kx)
    extend((vl, v, vr), vx)
    unit = eye(HD)
    for e in range(6):
        block = slice(e * TILE, (e + 1) * TILE)
        kt[:, block] = dot_nt(unit, kx[block]).astype(jnp.bfloat16)
    products = g[...].astype(jnp.float32) * att[...].astype(jnp.float32)
    ones = jnp.ones((8, HD), jnp.float32)
    deltas = dot_nt(ones, products, lax.Precision.HIGHEST)[0:1]
    totals = stat[0, 0:1, :]
    for e in range(6):
        keys = kx[e * TILE : (e + 1) * TILE]
        values = vx[e * TILE : (e + 1) * TILE]
        tiles = [i for i in range(TILES_DEV) if 0 <= e - i < WIN]
        dk = jnp.zeros((TILE, HD), jnp.float32)
        dv = jnp.zeros((TILE, HD), jnp.float32)
        for i in tiles:
            rows = slice(i * TILE, (i + 1) * TILE)
            ok = allowed(ids, mask, i, e - i)
            level = jnp.where(ok, totals[:, rows], jnp.float32(-NEG))
            scores = dot_nt(keys, q[rows]) * jnp.float32(SCALING * LOG2E)
            weight = jnp.exp2(scores - level)
            probs = dot_nt(values, g[rows])
            ds = (weight * (probs - deltas[:, rows])).astype(jnp.bfloat16)
            dsx[e * TILE : (e + 1) * TILE, rows] = ds
            dk = dk + dot_nn(ds, q[rows])
            dv = dv + dot_nn(weight.astype(jnp.bfloat16), g[rows])
        dk = dk * jnp.float32(SCALING)
        part = (e % 2) * TILE
        target = (dl, do, dr)[e // 2]
        target[part : part + TILE] = dk.astype(target.dtype)
        target[TOK + part : TOK + part + TILE] = dv.astype(target.dtype)
    wide = eye(TILE)
    for i in range(TILES_DEV):
        rows = slice(i * TILE, (i + 1) * TILE)
        window = slice(i * TILE, (i + WIN) * TILE)
        turned = dot_nn(kt[:, window], dsx[window, rows]) * jnp.float32(SCALING)
        dq[rows] = dot_nt(wide, turned.astype(jnp.bfloat16)).astype(jnp.bfloat16)


def attention_specs():
    narrow = pl.BlockSpec((TOK, HD), lambda h, *_: (0, h))
    second = pl.BlockSpec((TOK, HD), lambda h, *_: (0, 2 + h))
    double = pl.BlockSpec((2 * TOK, HD), lambda h, *_: (0, h))
    stat = pl.BlockSpec((1, 8, TOK), lambda h, *_: (h, 0, 0))
    pieces = [narrow, narrow, narrow, second, narrow, second]
    return narrow, double, stat, pieces


def attention_forward(ids, mask, q, keys, values):
    narrow, _, stat, pieces = attention_specs()
    return pl.pallas_call(
        forward_kernel,
        grid_spec=pltpu.PrefetchScalarGridSpec(
            num_scalar_prefetch=2,
            grid=(2,),
            in_specs=[narrow] + pieces,
            out_specs=[narrow, narrow, stat],
            scratch_shapes=[pltpu.VMEM((3 * TOK, HD), jnp.bfloat16)] * 2,
        ),
        out_shape=[
            jax.ShapeDtypeStruct((TOK, 2 * HD), jnp.bfloat16),
            jax.ShapeDtypeStruct((TOK, 2 * HD), jnp.bfloat16),
            jax.ShapeDtypeStruct((2, 8, TOK), jnp.float32),
        ],
        cost_estimate=pl.CostEstimate(
            flops=700_000_000, bytes_accessed=2_400_000, transcendentals=1_300_000
        ),
        compiler_params=pltpu.CompilerParams(vmem_limit_bytes=VMEM_BYTES),
        name="attention_forward",
    )(ids, mask, q, *keys, *values)


def attention_backward(ids, mask, q, keys, values, g, att, stats):
    narrow, double, stat, pieces = attention_specs()
    return pl.pallas_call(
        backward_kernel,
        grid_spec=pltpu.PrefetchScalarGridSpec(
            num_scalar_prefetch=2,
            grid=(2,),
            in_specs=[narrow] + pieces + [narrow, narrow, stat],
            out_specs=[narrow, double, double, double],
            scratch_shapes=[pltpu.VMEM((3 * TOK, HD), jnp.bfloat16)] * 2
            + [
                pltpu.VMEM((3 * TOK, TOK), jnp.bfloat16),
                pltpu.VMEM((HD, 3 * TOK), jnp.bfloat16),
            ],
        ),
        out_shape=[
            jax.ShapeDtypeStruct((TOK, 2 * HD), jnp.bfloat16),
            jax.ShapeDtypeStruct((2 * TOK, 2 * HD), jnp.bfloat16),
            jax.ShapeDtypeStruct((2 * TOK, 2 * HD), jnp.float32),
            jax.ShapeDtypeStruct((2 * TOK, 2 * HD), jnp.bfloat16),
        ],
        cost_estimate=pl.CostEstimate(
            flops=1_800_000_000, bytes_accessed=5_000_000, transcendentals=1_300_000
        ),
        compiler_params=pltpu.CompilerParams(vmem_limit_bytes=VMEM_BYTES),
        name="attention_backward",
    )(ids, mask, q, *keys, *values, g, att, stats)


def pack_kernel(ids, w, out):
    unit = eye(HD)
    for t in range(GROUP // HD):
        turned = dot_nt(unit, w[:, t * HD : (t + 1) * HD]).astype(jnp.bfloat16)
        for half in range(2):
            row = t * HD + half * 64
            out[0, row // CB, 0, row % CB : row % CB + 64] = turned[half * 64 : half * 64 + 64]


def pack_weights(ids, w):
    return pl.pallas_call(
        pack_kernel,
        grid_spec=pltpu.PrefetchScalarGridSpec(
            num_scalar_prefetch=1,
            grid=(GROUPS,),
            in_specs=[pl.BlockSpec((HD, GROUP), lambda s, ids: (ids[1], s))],
            out_specs=pl.BlockSpec((1, 2, 1, CB, HD), lambda s, ids: (s // 4, 0, s % 4, 0, 0)),
        ),
        out_shape=jax.ShapeDtypeStruct((2, 2, 4, CB, HD), jnp.bfloat16),
        cost_estimate=pl.CostEstimate(
            flops=170_000_000, bytes_accessed=2_600_000, transcendentals=0
        ),
        compiler_params=pltpu.CompilerParams(vmem_limit_bytes=VMEM_BYTES),
        name="pack_weights",
    )(ids, w)


def project_kernel(ids, mine, other, a0, a1, a2, a3, o0, o1, o2, o3, wide):
    core = ids[1]
    here = ids[2]
    far = ids[3]
    for p, out in ((2, o2), (1, o1), (3, o3), (0, o0)):
        total = jnp.zeros((CB, TOK), jnp.float32)
        for r, a in enumerate((a0, a1, a2, a3)):
            source = here ^ r
            block = far ^ p
            wide[p, r, :, pl.ds(pl.multiple_of(core * HD, HD), HD)] = mine[source, block]
            wide[p, r, :, pl.ds(pl.multiple_of((1 - core) * HD, HD), HD)] = other[source, block]
            total = total + dot_nt(wide[p, r], a[...])
        out[...] = total.astype(jnp.bfloat16)


def project(ids, mine, other, gathered):
    whole = pl.BlockSpec(memory_space=pltpu.VMEM)
    return pl.pallas_call(
        project_kernel,
        in_specs=[pl.BlockSpec(memory_space=pltpu.SMEM)] + [whole] * 6,
        out_specs=[whole] * 4,
        scratch_shapes=[pltpu.VMEM((4, 4, CB, 2 * HD), jnp.bfloat16)],
        out_shape=[jax.ShapeDtypeStruct((CB, TOK), jnp.bfloat16)] * 4,
        cost_estimate=pl.CostEstimate(
            flops=1_340_000_000, bytes_accessed=5_000_000, transcendentals=0
        ),
        compiler_params=pltpu.CompilerParams(vmem_limit_bytes=VMEM_BYTES),
        name="project",
    )(ids, mine, other, *gathered)


def upstream_kernel(ids, up, w, att, g, mine, other, turned, pair, acc):
    core = ids[1]
    step = pl.program_id(0)

    @pl.when(step == 0)
    def _():
        turned[...] = dot_nt(eye(2 * HD), att[...]).astype(jnp.bfloat16)
        acc[...] = jnp.zeros_like(acc)

    acc[...] += dot_nt(up[...], w[...])
    grad = dot_nn(turned[...], up[...]).astype(jnp.bfloat16)
    unit = eye(HD)
    for t in range(GROUP // HD):
        block = slice(t * HD, (t + 1) * HD)
        pair[block] = dot_nt(unit, grad[:, block]).astype(jnp.bfloat16)
    mine[0] = pair[pl.ds(pl.multiple_of(core * CB, CB), CB)]
    other[0] = pair[pl.ds(pl.multiple_of((1 - core) * CB, CB), CB)]

    @pl.when(step == GROUPS - 1)
    def _():
        g[...] = acc[...].astype(jnp.bfloat16)


def use_upstream(ids, up, w, att):
    part = pl.BlockSpec((1, CB, 2 * HD), lambda s, ids: (s ^ ids[4], 0, 0))
    whole = pl.BlockSpec((TOK, 2 * HD), lambda s, ids: (0, 0))
    return pl.pallas_call(
        upstream_kernel,
        grid_spec=pltpu.PrefetchScalarGridSpec(
            num_scalar_prefetch=1,
            grid=(GROUPS,),
            in_specs=[
                pl.BlockSpec((TOK, GROUP), lambda s, ids: (0, s)),
                pl.BlockSpec((2 * HD, GROUP), lambda s, ids: (0, s)),
                whole,
            ],
            out_specs=[whole, part, part],
            scratch_shapes=[
                pltpu.VMEM((2 * HD, TOK), jnp.bfloat16),
                pltpu.VMEM((GROUP, 2 * HD), jnp.bfloat16),
                pltpu.VMEM((TOK, 2 * HD), jnp.float32),
            ],
        ),
        out_shape=[jax.ShapeDtypeStruct((TOK, 2 * HD), jnp.bfloat16)]
        + [jax.ShapeDtypeStruct((GROUPS, CB, 2 * HD), jnp.bfloat16)] * 2,
        cost_estimate=pl.CostEstimate(
            flops=3_000_000_000, bytes_accessed=11_000_000, transcendentals=0
        ),
        compiler_params=pltpu.CompilerParams(vmem_limit_bytes=VMEM_BYTES),
        name="use_upstream",
    )(ids, up, w, att)


def merge_kernel(mine, near, *outs):
    for p, out in enumerate(outs):
        total = mine[p].astype(jnp.float32) + near[p].astype(jnp.float32)
        out[...] = total.astype(jnp.bfloat16)


def merge(mine, near):
    whole = pl.BlockSpec(memory_space=pltpu.VMEM)
    return pl.pallas_call(
        merge_kernel,
        in_specs=[whole] * 2,
        out_specs=[whole] * PLANE,
        out_shape=[jax.ShapeDtypeStruct((CB, 2 * HD), jnp.bfloat16)] * PLANE,
        cost_estimate=pl.CostEstimate(
            flops=1_000_000, bytes_accessed=4_000_000, transcendentals=0
        ),
        compiler_params=pltpu.CompilerParams(vmem_limit_bytes=VMEM_BYTES),
        name="merge",
    )(mine, near)


def gram_kernel(*refs):
    parts, (left, right) = refs[:PLANE], refs[PLANE:]
    highest = lax.Precision.HIGHEST
    total = parts[0][...].astype(jnp.float32)
    for part in parts[1:]:
        total = total + part[...].astype(jnp.float32)
    for h in range(2):
        block = total[:, h * HD : (h + 1) * HD]
        squares = jnp.sum(block * block, axis=0, keepdims=True)
        trace = jnp.sum(squares, axis=1, keepdims=True)
        inverse = 1.0 / (trace + epsilon)
        turned = block.T
        left[h, 0] = dot_nt(turned, turned, highest) * (inverse * HD)
        right[h, 0] = dot_nt(block, block, highest) * (inverse * CB)


def gram(parts):
    whole = pl.BlockSpec(memory_space=pltpu.VMEM)
    return pl.pallas_call(
        gram_kernel,
        in_specs=[whole] * PLANE,
        out_specs=[whole] * 2,
        out_shape=[
            jax.ShapeDtypeStruct((2, 1, HD, HD), jnp.float32),
            jax.ShapeDtypeStruct((2, 1, CB, CB), jnp.float32),
        ],
        cost_estimate=pl.CostEstimate(
            flops=400_000_000, bytes_accessed=2_000_000, transcendentals=0
        ),
        compiler_params=pltpu.CompilerParams(vmem_limit_bytes=VMEM_BYTES),
        name="gram",
    )(*parts)


def pair_kernel(k, v, out, sems):
    first = pltpu.make_async_copy(k, out.at[:, 0 : 2 * HD], sems.at[0])
    second = pltpu.make_async_copy(v, out.at[:, 2 * HD : 4 * HD], sems.at[1])
    first.start()
    second.start()
    first.wait()
    second.wait()


def pair_up(k, v):
    return pl.pallas_call(
        pair_kernel,
        in_specs=[pl.BlockSpec(memory_space=pl.ANY)] * 2,
        out_specs=pl.BlockSpec(memory_space=pltpu.VMEM),
        scratch_shapes=[pltpu.SemaphoreType.DMA((2,))],
        out_shape=jax.ShapeDtypeStruct((TOK, 4 * HD), jnp.bfloat16),
        cost_estimate=pl.CostEstimate(flops=0, bytes_accessed=1_000_000, transcendentals=0),
        compiler_params=pltpu.CompilerParams(vmem_limit_bytes=VMEM_BYTES),
        name="pair_up",
    )(k, v)


def in_hbm(x):
    return pltpu.with_memory_space_constraint(x, pltpu.HBM)


def local(query_states, key_states, value_states, out_weight, upstream, tile_mask):
    frame = lax.axis_index(FRAME).astype(jnp.int32)
    core = lax.axis_index("core").astype(jnp.int32)
    here = lax.axis_index(NEAR).astype(jnp.int32)
    far = lax.axis_index("zq").astype(jnp.int32)
    plane = lax.axis_index(("xlo", "y")).astype(jnp.int32)
    ids = jnp.stack([frame, core, here, far, plane])
    frames = lax.axis_size(FRAME)
    up = [(i, i + 1) for i in range(frames - 1)]
    down = [(j, i) for i, j in up]
    cores = [(0, 1), (1, 0)]
    mask = tile_mask.T
    query_states = in_hbm(query_states)
    key_states = in_hbm(key_states)
    value_states = in_hbm(value_states)
    out_weight = in_hbm(out_weight)
    upstream = in_hbm(upstream)

    both = pair_up(key_states, value_states)
    before = lax.ppermute(both, FRAME, up)
    after = lax.ppermute(both, FRAME, down)
    keys = (before, key_states, after)
    values = (before, value_states, after)

    strips = pack_weights(ids, out_weight).reshape(4, 4, CB, HD)
    strips_mine = lax.all_to_all(strips, NEAR, 0, 0, tiled=True)
    strips_other = lax.ppermute(strips_mine, "core", cores)

    attended, att, stats = attention_forward(ids, mask, query_states, keys, values)
    gathered = [att] * 4
    for p in (3, 2, 1):
        pairs = [(i, i ^ p) for i in range(4)]
        gathered[p] = lax.ppermute(att, NEAR, pairs)

    grad_attended, half_mine, half_other = use_upstream(ids, upstream, out_weight, att)
    half_near = lax.ppermute(half_other, "core", cores)
    halves = merge(half_mine, half_near)
    grad_parts = [halves[0]]
    for p in (6, 7, 5, 4, 2, 3, 1):
        pairs = [(i, i ^ p) for i in range(PLANE)]
        grad_parts.append(lax.ppermute(halves[p], ("xlo", "y"), pairs))

    partials = project(ids, strips_mine, strips_other, gathered)
    projected = partials[0].astype(jnp.float32)
    for p in (2, 1, 3):
        pairs = [(i, i ^ p) for i in range(4)]
        arrived = lax.ppermute(partials[p], "zq", pairs)
        projected = projected + arrived.astype(jnp.float32)
    projected = projected.astype(jnp.bfloat16).T

    grad_query, left, own, right = attention_backward(
        ids, mask, query_states, keys, values, grad_attended, att, stats
    )
    from_right = lax.ppermute(left, FRAME, down)
    from_left = lax.ppermute(right, FRAME, up)
    summed = own + from_right.astype(jnp.float32) + from_left.astype(jnp.float32)
    grad_key = summed[:TOK].astype(jnp.bfloat16)
    grad_value = summed[TOK:].astype(jnp.bfloat16)

    gram_left, gram_right = gram(grad_parts)
    return (attended, projected, grad_query, grad_key, grad_value, gram_left, gram_right)


def solution(mesh):
    fine = Mesh(mesh.devices.reshape(2, 4, 2, 2, 4, 2), FRAME + HEAD)
    placed = (
        P(FRAME, HEAD),
        P(FRAME, HEAD),
        P(FRAME, HEAD),
        P(HEAD, None),
        P(FRAME, None),
        P(),
    )
    return jax.shard_map(
        local,
        mesh=fine,
        in_specs=placed,
        out_specs=(
            P(FRAME, HEAD),
            P(FRAME, HEAD),
            P(FRAME, HEAD),
            P(FRAME, HEAD),
            P(FRAME, HEAD),
            P(HEAD, FRAME, None, None),
            P(HEAD, FRAME, None, None),
        ),
        check_vma=False,
    )
```

```python
import functools
import math

import jax
import jax.numpy as jnp
from jax import lax
from jax.experimental import pallas as pl
from jax.experimental.pallas import tpu as pltpu
from jax.sharding import Mesh
from jax.sharding import PartitionSpec as P


D = 5120
HD = 128
TILE = 256
TILES_DEV = 2
CB = 320
TOK = 512
NT = 32
WIN = 5
GROUP = 2 * CB
STRIP = 4 * CB
STRIPS = D // STRIP
FRAME = ("xlo", "y", "core")
HEAD = ("xhi", "zq", "zp")
NEAR = ("xhi", "zp")


epsilon = 1e-06
SCALING = 1.0 / math.sqrt(HD)
LOG2E = 1.0 / math.log(2.0)
NEG = -1e30
VMEM_BYTES = 16 * 1024 * 1024
PLANE = 8
ORDER = (2, 1, 3, 0)


def dot_nt(a, b, precision=None):
    return lax.dot_general(
        a, b, (((1,), (1,)), ((), ())), precision=precision, preferred_element_type=jnp.float32
    )


def dot_nn(a, b):
    return jnp.dot(a, b, preferred_element_type=jnp.float32)


def eye(n):
    rows = lax.broadcasted_iota(jnp.int32, (n, n), 0)
    cols = lax.broadcasted_iota(jnp.int32, (n, n), 1)
    return (rows == cols).astype(jnp.float32).astype(jnp.bfloat16)


def allowed(ids, mask, i, j):
    tile = ids[0] * TILES_DEV + i
    key_tile = tile + (j - 2)
    return (mask[j, tile] == 1) & (key_tile >= 0) & (key_tile < NT)


def extend(k, v, before, after, kx, vx):
    head = pl.program_id(0)
    lanes = pl.ds(pl.multiple_of(head * HD, HD), HD)
    value_lanes = pl.ds(pl.multiple_of((2 + head) * HD, HD), HD)
    kx[0:TOK] = before[:, lanes]
    kx[TOK : 2 * TOK] = k[...]
    kx[2 * TOK : 3 * TOK] = after[:, lanes]
    vx[0:TOK] = before[:, value_lanes]
    vx[TOK : 2 * TOK] = v[...]
    vx[2 * TOK : 3 * TOK] = after[:, value_lanes]
    return lanes


def forward_kernel(ids, mask, q, k, v, before, after, att, copy, stat, kx, vx):
    head = pl.program_id(0)
    lanes = extend(k, v, before, after, kx, vx)
    first_lane = lax.broadcasted_iota(jnp.int32, (8, HD), 1) == 0
    pick = jnp.where(first_lane, jnp.float32(1), jnp.float32(0))
    for i in range(TILES_DEV):
        rows = slice(i * TILE, (i + 1) * TILE)
        parts = []
        for j in range(WIN):
            keys = kx[(i + j) * TILE : (i + j + 1) * TILE]
            part = dot_nt(q[rows], keys) * jnp.float32(SCALING * LOG2E)
            parts.append(jnp.where(allowed(ids, mask, i, j), part, jnp.float32(NEG)))
        peak = parts[0]
        for part in parts[1:]:
            peak = jnp.maximum(peak, part)
        peak = jnp.max(peak, axis=1, keepdims=True)
        out = jnp.zeros((TILE, HD), jnp.float32)
        total = jnp.zeros((TILE, TILE), jnp.float32)
        for j in range(WIN):
            weight = jnp.exp2(parts[j] - peak)
            total = total + weight
            values = vx[(i + j) * TILE : (i + j + 1) * TILE]
            out = out + dot_nn(weight.astype(jnp.bfloat16), values)
        total = jnp.sum(total, axis=1, keepdims=True)
        result = (out / total).astype(jnp.bfloat16)
        att[rows] = result
        copy[rows, lanes] = result
        log_total = peak + jnp.log(total) * jnp.float32(LOG2E)
        spread = jnp.broadcast_to(log_total, (TILE, HD))
        stat[head, :, rows] = dot_nt(pick, spread, lax.Precision.HIGHEST)


def backward_kernel(
    ids, mask, q, k, v, before, after, grads, att, stat, dq, dl, do, dr, kx, vx, g, dsx, kt
):
    head = pl.program_id(0)
    lanes = extend(k, v, before, after, kx, vx)
    g[...] = grads[:, lanes]
    unit = eye(HD)
    for e in range(6):
        block = slice(e * TILE, (e + 1) * TILE)
        kt[:, block] = dot_nt(unit, kx[block]).astype(jnp.bfloat16)
    products = g[...].astype(jnp.float32) * att[:, lanes].astype(jnp.float32)
    ones = jnp.ones((8, HD), jnp.float32)
    deltas = dot_nt(ones, products, lax.Precision.HIGHEST)[0:1]
    totals = stat[head, 0:1, :]
    for e in range(6):
        keys = kx[e * TILE : (e + 1) * TILE]
        values = vx[e * TILE : (e + 1) * TILE]
        tiles = [i for i in range(TILES_DEV) if 0 <= e - i < WIN]
        dk = jnp.zeros((TILE, HD), jnp.float32)
        dv = jnp.zeros((TILE, HD), jnp.float32)
        for i in tiles:
            rows = slice(i * TILE, (i + 1) * TILE)
            ok = allowed(ids, mask, i, e - i)
            level = jnp.where(ok, totals[:, rows], jnp.float32(-NEG))
            scores = dot_nt(keys, q[rows]) * jnp.float32(SCALING * LOG2E)
            weight = jnp.exp2(scores - level)
            probs = dot_nt(values, g[rows])
            ds = (weight * (probs - deltas[:, rows])).astype(jnp.bfloat16)
            dsx[e * TILE : (e + 1) * TILE, rows] = ds
            dk = dk + dot_nn(ds, q[rows])
            dv = dv + dot_nn(weight.astype(jnp.bfloat16), g[rows])
        dk = dk * jnp.float32(SCALING)
        part = (e % 2) * TILE
        target = (dl, do, dr)[e // 2]
        target[part : part + TILE, lanes] = dk.astype(target.dtype)
        target[TOK + part : TOK + part + TILE, lanes] = dv.astype(target.dtype)
    wide = eye(TILE)
    for i in range(TILES_DEV):
        rows = slice(i * TILE, (i + 1) * TILE)
        window = slice(i * TILE, (i + WIN) * TILE)
        turned = dot_nn(kt[:, window], dsx[window, rows]) * jnp.float32(SCALING)
        dq[rows] = dot_nt(wide, turned.astype(jnp.bfloat16)).astype(jnp.bfloat16)


def attention_specs():
    narrow = pl.BlockSpec((TOK, HD), lambda h, *_: (0, h))
    whole = pl.BlockSpec(memory_space=pltpu.VMEM)
    return narrow, whole


def attention_forward(ids, mask, q, k, v, before, after):
    narrow, whole = attention_specs()
    return pl.pallas_call(
        forward_kernel,
        grid_spec=pltpu.PrefetchScalarGridSpec(
            num_scalar_prefetch=2,
            grid=(2,),
            in_specs=[narrow] * 3 + [whole] * 2,
            out_specs=[narrow, whole, whole],
            scratch_shapes=[pltpu.VMEM((3 * TOK, HD), jnp.bfloat16)] * 2,
        ),
        out_shape=[
            jax.ShapeDtypeStruct((TOK, 2 * HD), jnp.bfloat16),
            jax.ShapeDtypeStruct((TOK, 2 * HD), jnp.bfloat16),
            jax.ShapeDtypeStruct((2, 8, TOK), jnp.float32),
        ],
        cost_estimate=pl.CostEstimate(
            flops=700_000_000, bytes_accessed=2_400_000, transcendentals=1_300_000
        ),
        compiler_params=pltpu.CompilerParams(vmem_limit_bytes=VMEM_BYTES),
        name="attention_forward",
    )(ids, mask, q, k, v, before, after)


def attention_backward(ids, mask, q, k, v, before, after, g, att, stats):
    narrow, whole = attention_specs()
    return pl.pallas_call(
        backward_kernel,
        grid_spec=pltpu.PrefetchScalarGridSpec(
            num_scalar_prefetch=2,
            grid=(2,),
            in_specs=[narrow] * 3 + [whole] * 5,
            out_specs=[narrow, whole, whole, whole],
            scratch_shapes=[pltpu.VMEM((3 * TOK, HD), jnp.bfloat16)] * 2
            + [
                pltpu.VMEM((TOK, HD), jnp.bfloat16),
                pltpu.VMEM((3 * TOK, TOK), jnp.bfloat16),
                pltpu.VMEM((HD, 3 * TOK), jnp.bfloat16),
            ],
        ),
        out_shape=[
            jax.ShapeDtypeStruct((TOK, 2 * HD), jnp.bfloat16),
            jax.ShapeDtypeStruct((2 * TOK, 2 * HD), jnp.bfloat16),
            jax.ShapeDtypeStruct((2 * TOK, 2 * HD), jnp.float32),
            jax.ShapeDtypeStruct((2 * TOK, 2 * HD), jnp.bfloat16),
        ],
        cost_estimate=pl.CostEstimate(
            flops=1_800_000_000, bytes_accessed=5_000_000, transcendentals=1_300_000
        ),
        compiler_params=pltpu.CompilerParams(vmem_limit_bytes=VMEM_BYTES),
        name="attention_backward",
    )(ids, mask, q, k, v, before, after, g, att, stats)


def pack_kernel(ids, w, o0, o1, o2, o3, buf, strips, sems):
    here = ids[2]
    far = ids[3]
    rows = pl.ds(pl.multiple_of(ids[1] * HD, HD), HD)
    copies = []
    for c in range(STRIPS):
        lanes = slice(c * STRIP, (c + 1) * STRIP)
        copies.append(pltpu.make_async_copy(w.at[rows, lanes], buf.at[:, lanes], sems.at[c]))
    for copy in copies:
        copy.start()
    for xhi in range(2):
        copies[2 * xhi].wait()
        copies[2 * xhi + 1].wait()
        for place, p in enumerate(ORDER):
            start = pl.multiple_of((xhi * 4 + (far ^ p)) * GROUP, GROUP)
            both = buf[:, pl.ds(start, GROUP)]
            for zp in range(2):
                strips[xhi * 2 + zp, :, place * CB : (place + 1) * CB] = both[
                    :, zp * CB : (zp + 1) * CB
                ]
    for p, out in enumerate((o0, o1, o2, o3)):
        out[...] = strips[here ^ p]


def pack_weights(ids, w):
    return pl.pallas_call(
        pack_kernel,
        in_specs=[pl.BlockSpec(memory_space=pltpu.SMEM), pl.BlockSpec(memory_space=pl.ANY)],
        out_specs=[pl.BlockSpec(memory_space=pltpu.VMEM)] * 4,
        scratch_shapes=[
            pltpu.VMEM((HD, D), jnp.bfloat16),
            pltpu.VMEM((4, HD, STRIP), jnp.bfloat16),
            pltpu.SemaphoreType.DMA((STRIPS,)),
        ],
        out_shape=[jax.ShapeDtypeStruct((HD, STRIP), jnp.bfloat16)] * 4,
        cost_estimate=pl.CostEstimate(flops=0, bytes_accessed=2_600_000, transcendentals=0),
        compiler_params=pltpu.CompilerParams(vmem_limit_bytes=VMEM_BYTES),
        name="pack_weights",
    )(ids, w)


def project_kernel(part, ids, *refs):
    mine, other, gathered, outs = refs[:4], refs[4:8], refs[8:12], refs[12:14]
    near, wide, flat = refs[14:]
    core = ids[1]
    lanes = slice(part * GROUP, (part + 1) * GROUP)
    for r in range(4):
        base = r * 2 * HD
        near[:, base : base + 2 * HD] = gathered[r][...]
        wide[pl.ds(pl.multiple_of(base + core * HD, HD), HD)] = mine[r][:, lanes]
        wide[pl.ds(pl.multiple_of(base + (1 - core) * HD, HD), HD)] = other[r][:, lanes]
    grown = dot_nn(near[...], wide[...]).astype(jnp.bfloat16)
    unit = eye(HD)
    for t in range(GROUP // HD):
        cols = slice(t * HD, (t + 1) * HD)
        flat[cols] = dot_nt(unit, grown[:, cols]).astype(jnp.bfloat16)
    for place, out in enumerate(outs):
        out[...] = flat[place * CB : (place + 1) * CB]


def project(ids, mine, other, gathered, part):
    whole = pl.BlockSpec(memory_space=pltpu.VMEM)
    return pl.pallas_call(
        functools.partial(project_kernel, part),
        in_specs=[pl.BlockSpec(memory_space=pltpu.SMEM)] + [whole] * 12,
        out_specs=[whole] * 2,
        scratch_shapes=[
            pltpu.VMEM((TOK, 8 * HD), jnp.bfloat16),
            pltpu.VMEM((8 * HD, GROUP), jnp.bfloat16),
            pltpu.VMEM((GROUP, TOK), jnp.bfloat16),
        ],
        out_shape=[jax.ShapeDtypeStruct((CB, TOK), jnp.bfloat16)] * 2,
        cost_estimate=pl.CostEstimate(
            flops=670_000_000, bytes_accessed=3_000_000, transcendentals=0
        ),
        compiler_params=pltpu.CompilerParams(vmem_limit_bytes=VMEM_BYTES),
        name="project",
    )(ids, *mine, *other, *gathered)


def weight_grad_kernel(ids, up, att, mine, other, buf, turned, sems):
    first_core = ids[1] == 0
    plane = ids[4]
    copies = [
        pltpu.make_async_copy(up.at[:, c * STRIP : (c + 1) * STRIP], buf.at[c], sems.at[c])
        for c in range(STRIPS)
    ]
    for copy in copies:
        copy.start()
    turned[...] = dot_nt(eye(2 * HD), att[...]).astype(jnp.bfloat16)
    for c, copy in enumerate(copies):
        copy.wait()
        halves = [
            dot_nn(turned[...], buf[c, :, base : base + GROUP]).astype(jnp.bfloat16)
            for base in (0, GROUP)
        ]
        lanes = pl.ds(pl.multiple_of((c ^ (plane // 2)) * GROUP, GROUP), GROUP)
        for target, low in ((mine, first_core), (other, jnp.logical_not(first_core))):
            first, second = (jnp.where(low, x[:, 0:CB], x[:, CB:GROUP]) for x in halves)
            straight = (plane & 1) == 0
            target[:, lanes] = jnp.concatenate(
                [jnp.where(straight, first, second), jnp.where(straight, second, first)], axis=1
            )


def weight_grad(ids, up, att):
    whole = pl.BlockSpec(memory_space=pltpu.VMEM)
    return pl.pallas_call(
        weight_grad_kernel,
        in_specs=[
            pl.BlockSpec(memory_space=pltpu.SMEM),
            pl.BlockSpec(memory_space=pl.ANY),
            whole,
        ],
        out_specs=[whole, whole],
        scratch_shapes=[
            pltpu.VMEM((STRIPS, TOK, STRIP), jnp.bfloat16),
            pltpu.VMEM((2 * HD, TOK), jnp.bfloat16),
            pltpu.SemaphoreType.DMA((STRIPS,)),
        ],
        out_shape=[jax.ShapeDtypeStruct((2 * HD, PLANE * CB), jnp.bfloat16)] * 2,
        cost_estimate=pl.CostEstimate(
            flops=1_700_000_000, bytes_accessed=8_000_000, transcendentals=0
        ),
        compiler_params=pltpu.CompilerParams(vmem_limit_bytes=VMEM_BYTES),
        name="weight_grad",
    )(ids, up, att)


def merge_kernel(mine, near, keep, send):
    for target, lanes in ((keep, slice(0, STRIP)), (send, slice(STRIP, 2 * STRIP))):
        total = mine[:, lanes].astype(jnp.float32) + near[:, lanes].astype(jnp.float32)
        target[...] = total.astype(jnp.bfloat16)


def merge(mine, near):
    whole = pl.BlockSpec(memory_space=pltpu.VMEM)
    return pl.pallas_call(
        merge_kernel,
        in_specs=[whole] * 2,
        out_specs=[whole] * 2,
        out_shape=[jax.ShapeDtypeStruct((2 * HD, STRIP), jnp.bfloat16)] * 2,
        cost_estimate=pl.CostEstimate(
            flops=1_000_000, bytes_accessed=4_000_000, transcendentals=0
        ),
        compiler_params=pltpu.CompilerParams(vmem_limit_bytes=VMEM_BYTES),
        name="merge",
    )(mine, near)


def merge_planes_kernel(keep, came, *outs):
    for p, out in enumerate(outs):
        lanes = slice(p * CB, (p + 1) * CB)
        total = keep[:, lanes].astype(jnp.float32) + came[:, lanes].astype(jnp.float32)
        out[...] = total.astype(jnp.bfloat16)


def merge_planes(keep, came):
    whole = pl.BlockSpec(memory_space=pltpu.VMEM)
    return pl.pallas_call(
        merge_planes_kernel,
        in_specs=[whole] * 2,
        out_specs=[whole] * 4,
        out_shape=[jax.ShapeDtypeStruct((2 * HD, CB), jnp.bfloat16)] * 4,
        cost_estimate=pl.CostEstimate(
            flops=1_000_000, bytes_accessed=2_000_000, transcendentals=0
        ),
        compiler_params=pltpu.CompilerParams(vmem_limit_bytes=VMEM_BYTES),
        name="merge_planes",
    )(keep, came)


def gram_kernel(*refs):
    parts, (left, right) = refs[:4], refs[4:]
    highest = lax.Precision.HIGHEST
    total = parts[0][...].astype(jnp.float32)
    for part in parts[1:]:
        total = total + part[...].astype(jnp.float32)
    for h in range(2):
        block = total[h * HD : (h + 1) * HD]
        squares = jnp.sum(block * block, axis=0, keepdims=True)
        trace = jnp.sum(squares, axis=1, keepdims=True)
        inverse = 1.0 / (trace + epsilon)
        turned = block.T
        left[h, 0] = dot_nt(block, block, highest) * (inverse * HD)
        right[h, 0] = dot_nt(turned, turned, highest) * (inverse * CB)


def gram(parts):
    whole = pl.BlockSpec(memory_space=pltpu.VMEM)
    return pl.pallas_call(
        gram_kernel,
        in_specs=[whole] * 4,
        out_specs=[whole] * 2,
        out_shape=[
            jax.ShapeDtypeStruct((2, 1, HD, HD), jnp.float32),
            jax.ShapeDtypeStruct((2, 1, CB, CB), jnp.float32),
        ],
        cost_estimate=pl.CostEstimate(
            flops=400_000_000, bytes_accessed=2_000_000, transcendentals=0
        ),
        compiler_params=pltpu.CompilerParams(vmem_limit_bytes=VMEM_BYTES),
        name="gram",
    )(*parts)


def pair_kernel(k, v, out, sems):
    first = pltpu.make_async_copy(k, out.at[:, 0 : 2 * HD], sems.at[0])
    second = pltpu.make_async_copy(v, out.at[:, 2 * HD : 4 * HD], sems.at[1])
    first.start()
    second.start()
    first.wait()
    second.wait()


def pair_up(k, v):
    return pl.pallas_call(
        pair_kernel,
        in_specs=[pl.BlockSpec(memory_space=pl.ANY)] * 2,
        out_specs=pl.BlockSpec(memory_space=pltpu.VMEM),
        scratch_shapes=[pltpu.SemaphoreType.DMA((2,))],
        out_shape=jax.ShapeDtypeStruct((TOK, 4 * HD), jnp.bfloat16),
        cost_estimate=pl.CostEstimate(flops=0, bytes_accessed=1_000_000, transcendentals=0),
        compiler_params=pltpu.CompilerParams(vmem_limit_bytes=VMEM_BYTES),
        name="pair_up",
    )(k, v)


def in_hbm(x):
    return pltpu.with_memory_space_constraint(x, pltpu.HBM)


def local(query_states, key_states, value_states, out_weight, upstream, tile_mask):
    frame = lax.axis_index(FRAME).astype(jnp.int32)
    core = lax.axis_index("core").astype(jnp.int32)
    here = lax.axis_index(NEAR).astype(jnp.int32)
    far = lax.axis_index("zq").astype(jnp.int32)
    plane = lax.axis_index(("xlo", "y")).astype(jnp.int32)
    ids = jnp.stack([frame, core, here, far, plane])
    frames = lax.axis_size(FRAME)
    up = [(i, i + 1) for i in range(frames - 1)]
    down = [(j, i) for i, j in up]
    cores = [(0, 1), (1, 0)]
    mask = tile_mask.T
    query_states = in_hbm(query_states)
    key_states = in_hbm(key_states)
    value_states = in_hbm(value_states)

    both = pair_up(key_states, value_states)
    before = lax.ppermute(both, FRAME, up)
    after = lax.ppermute(both, FRAME, down)

    grad_attended = lax.dot_general(
        upstream, out_weight, (((1,), (1,)), ((), ())), preferred_element_type=jnp.float32
    ).astype(jnp.bfloat16)
    strips_mine = list(pack_weights(ids, in_hbm(out_weight)))
    for p in (3, 2, 1):
        pairs = [(i, i ^ p) for i in range(4)]
        strips_mine[p] = lax.ppermute(strips_mine[p], NEAR, pairs)
    strips_other = []
    for p in range(4):
        strips_other.append(lax.ppermute(strips_mine[p], "core", cores))

    attended, att, stats = attention_forward(
        ids, mask, query_states, key_states, value_states, before, after
    )
    gathered = [att] * 4
    for p in (3, 2, 1):
        pairs = [(i, i ^ p) for i in range(4)]
        gathered[p] = lax.ppermute(att, NEAR, pairs)

    half_mine, half_other = weight_grad(ids, in_hbm(upstream), att)
    half_near = lax.ppermute(half_other, "core", cores)
    keep, send = merge(half_mine, half_near)
    came = lax.ppermute(send, "xlo", cores)
    quarters = merge_planes(keep, came)
    grad_parts = [quarters[0]]
    for p in (2, 3, 1):
        pairs = [(i, i ^ p) for i in range(4)]
        grad_parts.append(lax.ppermute(quarters[p], "y", pairs))

    partials = []
    arrived = []
    for place, p in enumerate(ORDER):
        if place % 2 == 0:
            partials += project(ids, strips_mine, strips_other, gathered, place // 2)
        if p:
            pairs = [(i, i ^ p) for i in range(4)]
            arrived.append(lax.ppermute(partials[place], "zq", pairs))
    projected = partials[3].astype(jnp.float32)
    for partial in arrived:
        projected = projected + partial.astype(jnp.float32)
    projected = projected.astype(jnp.bfloat16).T

    grad_query, left, own, right = attention_backward(
        ids,
        mask,
        query_states,
        key_states,
        value_states,
        before,
        after,
        grad_attended,
        att,
        stats,
    )
    from_right = lax.ppermute(left, FRAME, down)
    from_left = lax.ppermute(right, FRAME, up)
    summed = own + from_right.astype(jnp.float32) + from_left.astype(jnp.float32)
    grad_key = summed[:TOK].astype(jnp.bfloat16)
    grad_value = summed[TOK:].astype(jnp.bfloat16)

    gram_left, gram_right = gram(grad_parts)
    return (attended, projected, grad_query, grad_key, grad_value, gram_left, gram_right)


def solution(mesh):
    fine = Mesh(mesh.devices.reshape(2, 4, 2, 2, 4, 2), FRAME + HEAD)
    placed = (
        P(FRAME, HEAD),
        P(FRAME, HEAD),
        P(FRAME, HEAD),
        P(HEAD, None),
        P(FRAME, None),
        P(),
    )
    return jax.shard_map(
        local,
        mesh=fine,
        in_specs=placed,
        out_specs=(
            P(FRAME, HEAD),
            P(FRAME, HEAD),
            P(FRAME, HEAD),
            P(FRAME, HEAD),
            P(FRAME, HEAD),
            P(HEAD, FRAME, None, None),
            P(HEAD, FRAME, None, None),
        ),
        check_vma=False,
    )
```

```python
import functools
import math

import jax
import jax.numpy as jnp
from jax import lax
from jax.experimental import pallas as pl
from jax.experimental.pallas import tpu as pltpu
from jax.sharding import Mesh
from jax.sharding import PartitionSpec as P


D = 5120
HD = 128
TILE = 256
TILES_DEV = 2
CB = 320
TOK = 512
NT = 32
WIN = 5
GROUP = 2 * CB
STRIP = 4 * CB
STRIPS = D // STRIP
FRAME = ("xlo", "y", "core")
HEAD = ("xhi", "zq", "zp")
NEAR = ("xhi", "zp")


epsilon = 1e-06
SCALING = 1.0 / math.sqrt(HD)
LOG2E = 1.0 / math.log(2.0)
NEG = -1e30
VMEM_BYTES = 16 * 1024 * 1024
PLANE = 8
ORDER = (2, 1, 3, 0)


def dot_nt(a, b, precision=None):
    return lax.dot_general(
        a, b, (((1,), (1,)), ((), ())), precision=precision, preferred_element_type=jnp.float32
    )


def dot_nn(a, b):
    return jnp.dot(a, b, preferred_element_type=jnp.float32)


def eye(n):
    rows = lax.broadcasted_iota(jnp.int32, (n, n), 0)
    cols = lax.broadcasted_iota(jnp.int32, (n, n), 1)
    return (rows == cols).astype(jnp.float32).astype(jnp.bfloat16)


def allowed(ids, mask, i, j):
    tile = ids[0] * TILES_DEV + i
    key_tile = tile + (j - 2)
    return (mask[j, tile] == 1) & (key_tile >= 0) & (key_tile < NT)


def extend(both, before, after, kx, vx):
    head = pl.program_id(0)
    lanes = pl.ds(pl.multiple_of(head * HD, HD), HD)
    value_lanes = pl.ds(pl.multiple_of((2 + head) * HD, HD), HD)
    kx[0:TOK] = before[:, lanes]
    kx[TOK : 2 * TOK] = both[:, lanes]
    kx[2 * TOK : 3 * TOK] = after[:, lanes]
    vx[0:TOK] = before[:, value_lanes]
    vx[TOK : 2 * TOK] = both[:, value_lanes]
    vx[2 * TOK : 3 * TOK] = after[:, value_lanes]
    return lanes


def forward_kernel(ids, mask, q, both, before, after, att, copy, stat, kx, vx):
    head = pl.program_id(0)
    lanes = extend(both, before, after, kx, vx)
    first_lane = lax.broadcasted_iota(jnp.int32, (8, HD), 1) == 0
    pick = jnp.where(first_lane, jnp.float32(1), jnp.float32(0))
    for i in range(TILES_DEV):
        rows = slice(i * TILE, (i + 1) * TILE)
        parts = []
        peak = jnp.full((TILE, HD), NEG, jnp.float32)
        for j in range(WIN):
            keys = kx[(i + j) * TILE : (i + j + 1) * TILE]
            part = dot_nt(q[rows, lanes], keys) * jnp.float32(SCALING * LOG2E)
            parts.append(part)
            high = jnp.maximum(part[:, 0:HD], part[:, HD : 2 * HD])
            high = jnp.where(allowed(ids, mask, i, j), high, jnp.float32(NEG))
            peak = jnp.maximum(peak, high)
        peak = jnp.max(peak, axis=1, keepdims=True)
        out = jnp.zeros((TILE, HD), jnp.float32)
        total = jnp.zeros((TILE, HD), jnp.float32)
        for j in range(WIN):
            level = jnp.where(allowed(ids, mask, i, j), peak, jnp.float32(-NEG))
            weight = jnp.exp2(parts[j] - level)
            total = total + (weight[:, 0:HD] + weight[:, HD : 2 * HD])
            values = vx[(i + j) * TILE : (i + j + 1) * TILE]
            out = out + dot_nn(weight.astype(jnp.bfloat16), values)
        total = jnp.sum(total, axis=1, keepdims=True)
        result = (out / total).astype(jnp.bfloat16)
        att[rows] = result
        copy[rows, lanes] = result
        log_total = peak + jnp.log(total) * jnp.float32(LOG2E)
        spread = jnp.broadcast_to(log_total, (TILE, HD))
        stat[head, :, rows] = dot_nt(pick, spread, lax.Precision.HIGHEST)


def backward_kernel(
    ids, mask, queries, both, before, after, grads, att, stat, dq, dl, do, dr, kx, vx, q, g, dsx, kt
):
    head = pl.program_id(0)
    lanes = extend(both, before, after, kx, vx)
    q[...] = queries[:, lanes]
    g[...] = grads[:, lanes]
    unit = eye(HD)
    for e in range(6):
        block = slice(e * TILE, (e + 1) * TILE)
        kt[:, block] = dot_nt(unit, kx[block]).astype(jnp.bfloat16)
    products = g[...].astype(jnp.float32) * att[:, lanes].astype(jnp.float32)
    ones = jnp.ones((8, HD), jnp.float32)
    deltas = dot_nt(ones, products, lax.Precision.HIGHEST)[0:1]
    totals = stat[head, 0:1, :]
    for e in range(6):
        keys = kx[e * TILE : (e + 1) * TILE]
        values = vx[e * TILE : (e + 1) * TILE]
        tiles = [i for i in range(TILES_DEV) if 0 <= e - i < WIN]
        dk = jnp.zeros((TILE, HD), jnp.float32)
        dv = jnp.zeros((TILE, HD), jnp.float32)
        for i in tiles:
            rows = slice(i * TILE, (i + 1) * TILE)
            ok = allowed(ids, mask, i, e - i)
            level = jnp.where(ok, totals[:, rows], jnp.float32(-NEG))
            scores = dot_nt(keys, q[rows]) * jnp.float32(SCALING * LOG2E)
            weight = jnp.exp2(scores - level)
            probs = dot_nt(values, g[rows])
            ds = (weight * (probs - deltas[:, rows])).astype(jnp.bfloat16)
            dsx[e * TILE : (e + 1) * TILE, rows] = ds
            dk = dk + dot_nn(ds, q[rows])
            dv = dv + dot_nn(weight.astype(jnp.bfloat16), g[rows])
        dk = dk * jnp.float32(SCALING)
        part = (e % 2) * TILE
        target = (dl, do, dr)[e // 2]
        target[part : part + TILE, lanes] = dk.astype(target.dtype)
        target[TOK + part : TOK + part + TILE, lanes] = dv.astype(target.dtype)
    wide = eye(TILE)
    for i in range(TILES_DEV):
        rows = slice(i * TILE, (i + 1) * TILE)
        window = slice(i * TILE, (i + WIN) * TILE)
        turned = dot_nn(kt[:, window], dsx[window, rows]) * jnp.float32(SCALING)
        dq[rows] = dot_nt(wide, turned.astype(jnp.bfloat16)).astype(jnp.bfloat16)


def attention_specs():
    narrow = pl.BlockSpec((TOK, HD), lambda h, *_: (0, h))
    whole = pl.BlockSpec(memory_space=pltpu.VMEM)
    return narrow, whole


def attention_forward(ids, mask, q, both, before, after):
    narrow, whole = attention_specs()
    return pl.pallas_call(
        forward_kernel,
        grid_spec=pltpu.PrefetchScalarGridSpec(
            num_scalar_prefetch=2,
            grid=(2,),
            in_specs=[whole] * 4,
            out_specs=[narrow, whole, whole],
            scratch_shapes=[pltpu.VMEM((3 * TOK, HD), jnp.bfloat16)] * 2,
        ),
        out_shape=[
            jax.ShapeDtypeStruct((TOK, 2 * HD), jnp.bfloat16),
            jax.ShapeDtypeStruct((TOK, 2 * HD), jnp.bfloat16),
            jax.ShapeDtypeStruct((2, 8, TOK), jnp.float32),
        ],
        cost_estimate=pl.CostEstimate(
            flops=700_000_000, bytes_accessed=2_400_000, transcendentals=1_300_000
        ),
        compiler_params=pltpu.CompilerParams(vmem_limit_bytes=VMEM_BYTES),
        name="attention_forward",
    )(ids, mask, q, both, before, after)


def attention_backward(ids, mask, q, both, before, after, g, att, stats):
    narrow, whole = attention_specs()
    return pl.pallas_call(
        backward_kernel,
        grid_spec=pltpu.PrefetchScalarGridSpec(
            num_scalar_prefetch=2,
            grid=(2,),
            in_specs=[whole] * 7,
            out_specs=[narrow, whole, whole, whole],
            scratch_shapes=[pltpu.VMEM((3 * TOK, HD), jnp.bfloat16)] * 2
            + [
                pltpu.VMEM((TOK, HD), jnp.bfloat16),
                pltpu.VMEM((TOK, HD), jnp.bfloat16),
                pltpu.VMEM((3 * TOK, TOK), jnp.bfloat16),
                pltpu.VMEM((HD, 3 * TOK), jnp.bfloat16),
            ],
        ),
        out_shape=[
            jax.ShapeDtypeStruct((TOK, 2 * HD), jnp.bfloat16),
            jax.ShapeDtypeStruct((2 * TOK, 2 * HD), jnp.bfloat16),
            jax.ShapeDtypeStruct((2 * TOK, 2 * HD), jnp.float32),
            jax.ShapeDtypeStruct((2 * TOK, 2 * HD), jnp.bfloat16),
        ],
        cost_estimate=pl.CostEstimate(
            flops=1_800_000_000, bytes_accessed=5_000_000, transcendentals=1_300_000
        ),
        compiler_params=pltpu.CompilerParams(vmem_limit_bytes=VMEM_BYTES),
        name="attention_backward",
    )(ids, mask, q, both, before, after, g, att, stats)


def pack_kernel(ids, w, o0, o1, o2, o3, buf, strips, sems):
    here = ids[2]
    far = ids[3]
    rows = pl.ds(pl.multiple_of(ids[1] * HD, HD), HD)
    copies = []
    for c in range(STRIPS):
        lanes = slice(c * STRIP, (c + 1) * STRIP)
        copies.append(pltpu.make_async_copy(w.at[rows, lanes], buf.at[:, lanes], sems.at[c]))
    for copy in copies:
        copy.start()
    for xhi in range(2):
        copies[2 * xhi].wait()
        copies[2 * xhi + 1].wait()
        for place, p in enumerate(ORDER):
            start = pl.multiple_of((xhi * 4 + (far ^ p)) * GROUP, GROUP)
            both = buf[:, pl.ds(start, GROUP)]
            for zp in range(2):
                strips[xhi * 2 + zp, :, place * CB : (place + 1) * CB] = both[
                    :, zp * CB : (zp + 1) * CB
                ]
    for p, out in enumerate((o0, o1, o2, o3)):
        out[...] = strips[here ^ p]


def pack_weights(ids, w):
    return pl.pallas_call(
        pack_kernel,
        in_specs=[pl.BlockSpec(memory_space=pltpu.SMEM), pl.BlockSpec(memory_space=pl.ANY)],
        out_specs=[pl.BlockSpec(memory_space=pltpu.VMEM)] * 4,
        scratch_shapes=[
            pltpu.VMEM((HD, D), jnp.bfloat16),
            pltpu.VMEM((4, HD, STRIP), jnp.bfloat16),
            pltpu.SemaphoreType.DMA((STRIPS,)),
        ],
        out_shape=[jax.ShapeDtypeStruct((HD, STRIP), jnp.bfloat16)] * 4,
        cost_estimate=pl.CostEstimate(flops=0, bytes_accessed=2_600_000, transcendentals=0),
        compiler_params=pltpu.CompilerParams(vmem_limit_bytes=VMEM_BYTES),
        name="pack_weights",
    )(ids, w)


def project_kernel(part, ids, *refs):
    mine, other, gathered, outs = refs[:4], refs[4:8], refs[8:12], refs[12:14]
    near, wide, flat = refs[14:]
    core = ids[1]
    lanes = slice(part * GROUP, (part + 1) * GROUP)
    for r in range(4):
        base = r * 2 * HD
        near[:, base : base + 2 * HD] = gathered[r][...]
        wide[pl.ds(pl.multiple_of(base + core * HD, HD), HD)] = mine[r][:, lanes]
        wide[pl.ds(pl.multiple_of(base + (1 - core) * HD, HD), HD)] = other[r][:, lanes]
    grown = dot_nn(near[...], wide[...]).astype(jnp.bfloat16)
    unit = eye(HD)
    for t in range(GROUP // HD):
        cols = slice(t * HD, (t + 1) * HD)
        flat[cols] = dot_nt(unit, grown[:, cols]).astype(jnp.bfloat16)
    for place, out in enumerate(outs):
        out[...] = flat[place * CB : (place + 1) * CB]


def project(ids, mine, other, gathered, part):
    whole = pl.BlockSpec(memory_space=pltpu.VMEM)
    return pl.pallas_call(
        functools.partial(project_kernel, part),
        in_specs=[pl.BlockSpec(memory_space=pltpu.SMEM)] + [whole] * 12,
        out_specs=[whole] * 2,
        scratch_shapes=[
            pltpu.VMEM((TOK, 8 * HD), jnp.bfloat16),
            pltpu.VMEM((8 * HD, GROUP), jnp.bfloat16),
            pltpu.VMEM((GROUP, TOK), jnp.bfloat16),
        ],
        out_shape=[jax.ShapeDtypeStruct((CB, TOK), jnp.bfloat16)] * 2,
        cost_estimate=pl.CostEstimate(
            flops=670_000_000, bytes_accessed=3_000_000, transcendentals=0
        ),
        compiler_params=pltpu.CompilerParams(vmem_limit_bytes=VMEM_BYTES),
        name="project",
    )(ids, *mine, *other, *gathered)


def weight_grad_kernel(ids, up, att, mine, other, buf, turned, sems):
    first_core = ids[1] == 0
    plane = ids[4]
    copies = [
        pltpu.make_async_copy(up.at[:, c * STRIP : (c + 1) * STRIP], buf.at[c], sems.at[c])
        for c in range(STRIPS)
    ]
    for copy in copies:
        copy.start()
    turned[...] = dot_nt(eye(2 * HD), att[...]).astype(jnp.bfloat16)
    for c, copy in enumerate(copies):
        copy.wait()
        halves = [
            dot_nn(turned[...], buf[c, :, base : base + GROUP]).astype(jnp.bfloat16)
            for base in (0, GROUP)
        ]
        lanes = pl.ds(pl.multiple_of((c ^ (plane // 2)) * GROUP, GROUP), GROUP)
        for target, low in ((mine, first_core), (other, jnp.logical_not(first_core))):
            first, second = (jnp.where(low, x[:, 0:CB], x[:, CB:GROUP]) for x in halves)
            straight = (plane & 1) == 0
            target[:, lanes] = jnp.concatenate(
                [jnp.where(straight, first, second), jnp.where(straight, second, first)], axis=1
            )


def weight_grad(ids, up, att):
    whole = pl.BlockSpec(memory_space=pltpu.VMEM)
    return pl.pallas_call(
        weight_grad_kernel,
        in_specs=[
            pl.BlockSpec(memory_space=pltpu.SMEM),
            pl.BlockSpec(memory_space=pl.ANY),
            whole,
        ],
        out_specs=[whole, whole],
        scratch_shapes=[
            pltpu.VMEM((STRIPS, TOK, STRIP), jnp.bfloat16),
            pltpu.VMEM((2 * HD, TOK), jnp.bfloat16),
            pltpu.SemaphoreType.DMA((STRIPS,)),
        ],
        out_shape=[jax.ShapeDtypeStruct((2 * HD, PLANE * CB), jnp.bfloat16)] * 2,
        cost_estimate=pl.CostEstimate(
            flops=1_700_000_000, bytes_accessed=8_000_000, transcendentals=0
        ),
        compiler_params=pltpu.CompilerParams(vmem_limit_bytes=VMEM_BYTES),
        name="weight_grad",
    )(ids, up, att)


def merge_kernel(mine, near, keep, send):
    for target, lanes in ((keep, slice(0, STRIP)), (send, slice(STRIP, 2 * STRIP))):
        total = mine[:, lanes].astype(jnp.float32) + near[:, lanes].astype(jnp.float32)
        target[...] = total.astype(jnp.bfloat16)


def merge(mine, near):
    whole = pl.BlockSpec(memory_space=pltpu.VMEM)
    return pl.pallas_call(
        merge_kernel,
        in_specs=[whole] * 2,
        out_specs=[whole] * 2,
        out_shape=[jax.ShapeDtypeStruct((2 * HD, STRIP), jnp.bfloat16)] * 2,
        cost_estimate=pl.CostEstimate(
            flops=1_000_000, bytes_accessed=4_000_000, transcendentals=0
        ),
        compiler_params=pltpu.CompilerParams(vmem_limit_bytes=VMEM_BYTES),
        name="merge",
    )(mine, near)


def merge_planes_kernel(keep, came, *outs):
    for p, out in enumerate(outs):
        lanes = slice(p * CB, (p + 1) * CB)
        total = keep[:, lanes].astype(jnp.float32) + came[:, lanes].astype(jnp.float32)
        out[...] = total.astype(jnp.bfloat16)


def merge_planes(keep, came):
    whole = pl.BlockSpec(memory_space=pltpu.VMEM)
    return pl.pallas_call(
        merge_planes_kernel,
        in_specs=[whole] * 2,
        out_specs=[whole] * 4,
        out_shape=[jax.ShapeDtypeStruct((2 * HD, CB), jnp.bfloat16)] * 4,
        cost_estimate=pl.CostEstimate(
            flops=1_000_000, bytes_accessed=2_000_000, transcendentals=0
        ),
        compiler_params=pltpu.CompilerParams(vmem_limit_bytes=VMEM_BYTES),
        name="merge_planes",
    )(keep, came)


def gram_kernel(*refs):
    parts, (left, right) = refs[:4], refs[4:]
    highest = lax.Precision.HIGHEST
    total = parts[0][...].astype(jnp.float32)
    for part in parts[1:]:
        total = total + part[...].astype(jnp.float32)
    for h in range(2):
        block = total[h * HD : (h + 1) * HD]
        squares = jnp.sum(block * block, axis=0, keepdims=True)
        trace = jnp.sum(squares, axis=1, keepdims=True)
        inverse = 1.0 / (trace + epsilon)
        turned = block.T
        left[h, 0] = dot_nt(block, block, highest) * (inverse * HD)
        right[h, 0] = dot_nt(turned, turned, highest) * (inverse * CB)


def gram(parts):
    whole = pl.BlockSpec(memory_space=pltpu.VMEM)
    return pl.pallas_call(
        gram_kernel,
        in_specs=[whole] * 4,
        out_specs=[whole] * 2,
        out_shape=[
            jax.ShapeDtypeStruct((2, 1, HD, HD), jnp.float32),
            jax.ShapeDtypeStruct((2, 1, CB, CB), jnp.float32),
        ],
        cost_estimate=pl.CostEstimate(
            flops=400_000_000, bytes_accessed=2_000_000, transcendentals=0
        ),
        compiler_params=pltpu.CompilerParams(vmem_limit_bytes=VMEM_BYTES),
        name="gram",
    )(*parts)


def pair_kernel(q, k, v, queries, both, sems):
    copies = [
        pltpu.make_async_copy(k, both.at[:, 0 : 2 * HD], sems.at[0]),
        pltpu.make_async_copy(v, both.at[:, 2 * HD : 4 * HD], sems.at[1]),
        pltpu.make_async_copy(q, queries, sems.at[2]),
    ]
    for copy in copies:
        copy.start()
    for copy in copies:
        copy.wait()


def pair_up(q, k, v):
    return pl.pallas_call(
        pair_kernel,
        in_specs=[pl.BlockSpec(memory_space=pl.ANY)] * 3,
        out_specs=[pl.BlockSpec(memory_space=pltpu.VMEM)] * 2,
        scratch_shapes=[pltpu.SemaphoreType.DMA((3,))],
        out_shape=[
            jax.ShapeDtypeStruct((TOK, 2 * HD), jnp.bfloat16),
            jax.ShapeDtypeStruct((TOK, 4 * HD), jnp.bfloat16),
        ],
        cost_estimate=pl.CostEstimate(flops=0, bytes_accessed=1_500_000, transcendentals=0),
        compiler_params=pltpu.CompilerParams(vmem_limit_bytes=VMEM_BYTES),
        name="pair_up",
    )(q, k, v)


def in_hbm(x):
    return pltpu.with_memory_space_constraint(x, pltpu.HBM)


def local(query_states, key_states, value_states, out_weight, upstream, tile_mask):
    frame = lax.axis_index(FRAME).astype(jnp.int32)
    core = lax.axis_index("core").astype(jnp.int32)
    here = lax.axis_index(NEAR).astype(jnp.int32)
    far = lax.axis_index("zq").astype(jnp.int32)
    plane = lax.axis_index(("xlo", "y")).astype(jnp.int32)
    ids = jnp.stack([frame, core, here, far, plane])
    frames = lax.axis_size(FRAME)
    up = [(i, i + 1) for i in range(frames - 1)]
    down = [(j, i) for i, j in up]
    cores = [(0, 1), (1, 0)]
    mask = tile_mask.T
    query_states = in_hbm(query_states)
    key_states = in_hbm(key_states)
    value_states = in_hbm(value_states)

    queries, both = pair_up(query_states, key_states, value_states)
    before = lax.ppermute(both, FRAME, up)
    after = lax.ppermute(both, FRAME, down)

    grad_attended = lax.dot_general(
        upstream, out_weight, (((1,), (1,)), ((), ())), preferred_element_type=jnp.float32
    ).astype(jnp.bfloat16)
    strips_mine = list(pack_weights(ids, in_hbm(out_weight)))
    for p in (3, 2, 1):
        pairs = [(i, i ^ p) for i in range(4)]
        strips_mine[p] = lax.ppermute(strips_mine[p], NEAR, pairs)
    strips_other = []
    for p in range(4):
        strips_other.append(lax.ppermute(strips_mine[p], "core", cores))

    attended, att, stats = attention_forward(ids, mask, queries, both, before, after)
    gathered = [att] * 4
    for p in (3, 2, 1):
        pairs = [(i, i ^ p) for i in range(4)]
        gathered[p] = lax.ppermute(att, NEAR, pairs)

    half_mine, half_other = weight_grad(ids, in_hbm(upstream), att)
    half_near = lax.ppermute(half_other, "core", cores)
    keep, send = merge(half_mine, half_near)
    came = lax.ppermute(send, "xlo", cores)
    quarters = merge_planes(keep, came)
    grad_parts = [quarters[0]]
    for p in (2, 3, 1):
        pairs = [(i, i ^ p) for i in range(4)]
        grad_parts.append(lax.ppermute(quarters[p], "y", pairs))

    partials = []
    arrived = []
    for place, p in enumerate(ORDER):
        if place % 2 == 0:
            partials += project(ids, strips_mine, strips_other, gathered, place // 2)
        if p:
            pairs = [(i, i ^ p) for i in range(4)]
            arrived.append(lax.ppermute(partials[place], "zq", pairs))
    projected = partials[3].astype(jnp.float32)
    for partial in arrived:
        projected = projected + partial.astype(jnp.float32)
    projected = projected.astype(jnp.bfloat16).T

    grad_query, left, own, right = attention_backward(
        ids,
        mask,
        queries,
        both,
        before,
        after,
        grad_attended,
        att,
        stats,
    )
    from_right = lax.ppermute(left, FRAME, down)
    from_left = lax.ppermute(right, FRAME, up)
    summed = own + from_right.astype(jnp.float32) + from_left.astype(jnp.float32)
    grad_key = summed[:TOK].astype(jnp.bfloat16)
    grad_value = summed[TOK:].astype(jnp.bfloat16)

    gram_left, gram_right = gram(grad_parts)
    return (attended, projected, grad_query, grad_key, grad_value, gram_left, gram_right)


def solution(mesh):
    fine = Mesh(mesh.devices.reshape(2, 4, 2, 2, 4, 2), FRAME + HEAD)
    placed = (
        P(FRAME, HEAD),
        P(FRAME, HEAD),
        P(FRAME, HEAD),
        P(HEAD, None),
        P(FRAME, None),
        P(),
    )
    return jax.shard_map(
        local,
        mesh=fine,
        in_specs=placed,
        out_specs=(
            P(FRAME, HEAD),
            P(FRAME, HEAD),
            P(FRAME, HEAD),
            P(FRAME, HEAD),
            P(FRAME, HEAD),
            P(HEAD, FRAME, None, None),
            P(HEAD, FRAME, None, None),
        ),
        check_vma=False,
    )
```

```python
import functools
import math

import jax
import jax.numpy as jnp
from jax import lax
from jax.experimental import pallas as pl
from jax.experimental.pallas import tpu as pltpu
from jax.sharding import Mesh
from jax.sharding import PartitionSpec as P


D = 5120
HD = 128
TILE = 256
TILES_DEV = 2
CB = 320
TOK = 512
NT = 32
WIN = 5
GROUP = 2 * CB
STRIP = 4 * CB
STRIPS = D // STRIP
FRAME = ("xlo", "y", "core")
HEAD = ("xhi", "zq", "zp")
NEAR = ("xhi", "zp")


epsilon = 1e-06
SCALING = 1.0 / math.sqrt(HD)
LOG2E = 1.0 / math.log(2.0)
NEG = -1e30
VMEM_BYTES = 16 * 1024 * 1024
PLANE = 8
ORDER = (2, 1, 3, 0)


def dot_nt(a, b, precision=None):
    return lax.dot_general(
        a, b, (((1,), (1,)), ((), ())), precision=precision, preferred_element_type=jnp.float32
    )


def dot_nn(a, b):
    return jnp.dot(a, b, preferred_element_type=jnp.float32)


def eye(n):
    rows = lax.broadcasted_iota(jnp.int32, (n, n), 0)
    cols = lax.broadcasted_iota(jnp.int32, (n, n), 1)
    return (rows == cols).astype(jnp.float32).astype(jnp.bfloat16)


def allowed(ids, mask, i, j):
    tile = ids[0] * TILES_DEV + i
    key_tile = tile + (j - 2)
    return (mask[j, tile] == 1) & (key_tile >= 0) & (key_tile < NT)


def extend(both, before, after, kx, vx):
    head = pl.program_id(0)
    lanes = pl.ds(pl.multiple_of(head * HD, HD), HD)
    value_lanes = pl.ds(pl.multiple_of((2 + head) * HD, HD), HD)
    kx[0:TOK] = before[:, lanes]
    kx[TOK : 2 * TOK] = both[:, lanes]
    kx[2 * TOK : 3 * TOK] = after[:, lanes]
    vx[0:TOK] = before[:, value_lanes]
    vx[TOK : 2 * TOK] = both[:, value_lanes]
    vx[2 * TOK : 3 * TOK] = after[:, value_lanes]
    return lanes


def forward_kernel(ids, mask, q, both, before, after, att, copy, stat, kx, vx):
    head = pl.program_id(0)
    lanes = extend(both, before, after, kx, vx)
    first_lane = lax.broadcasted_iota(jnp.int32, (8, HD), 1) == 0
    pick = jnp.where(first_lane, jnp.float32(1), jnp.float32(0))
    for i in range(TILES_DEV):
        rows = slice(i * TILE, (i + 1) * TILE)
        parts = []
        peak = jnp.full((TILE, HD), NEG, jnp.float32)
        for j in range(WIN):
            keys = kx[(i + j) * TILE : (i + j + 1) * TILE]
            part = dot_nt(q[rows, lanes], keys) * jnp.float32(SCALING * LOG2E)
            parts.append(part)
            high = jnp.maximum(part[:, 0:HD], part[:, HD : 2 * HD])
            high = jnp.where(allowed(ids, mask, i, j), high, jnp.float32(NEG))
            peak = jnp.maximum(peak, high)
        peak = jnp.max(peak, axis=1, keepdims=True)
        out = jnp.zeros((TILE, HD), jnp.float32)
        total = jnp.zeros((TILE, HD), jnp.float32)
        for j in range(WIN):
            level = jnp.where(allowed(ids, mask, i, j), peak, jnp.float32(-NEG))
            weight = jnp.exp2(parts[j] - level)
            total = total + (weight[:, 0:HD] + weight[:, HD : 2 * HD])
            values = vx[(i + j) * TILE : (i + j + 1) * TILE]
            out = out + dot_nn(weight.astype(jnp.bfloat16), values)
        total = jnp.sum(total, axis=1, keepdims=True)
        result = (out / total).astype(jnp.bfloat16)
        att[rows] = result
        copy[rows, lanes] = result
        log_total = peak + jnp.log(total) * jnp.float32(LOG2E)
        spread = jnp.broadcast_to(log_total, (TILE, HD))
        stat[head, :, rows] = dot_nt(pick, spread, lax.Precision.HIGHEST)


def backward_kernel(
    ids, mask, queries, both, before, after, grads, att, stat, dq, dl, do, dr, kx, vx, q, g, dsx, kt
):
    head = pl.program_id(0)
    lanes = extend(both, before, after, kx, vx)
    q[...] = queries[:, lanes]
    g[...] = grads[:, lanes]
    unit = eye(HD)
    for e in range(6):
        block = slice(e * TILE, (e + 1) * TILE)
        kt[:, block] = dot_nt(unit, kx[block]).astype(jnp.bfloat16)
    products = g[...].astype(jnp.float32) * att[:, lanes].astype(jnp.float32)
    ones = jnp.ones((8, HD), jnp.float32)
    deltas = dot_nt(ones, products, lax.Precision.HIGHEST)[0:1]
    totals = stat[head, 0:1, :]
    for e in range(6):
        keys = kx[e * TILE : (e + 1) * TILE]
        values = vx[e * TILE : (e + 1) * TILE]
        tiles = [i for i in range(TILES_DEV) if 0 <= e - i < WIN]
        dk = jnp.zeros((TILE, HD), jnp.float32)
        dv = jnp.zeros((TILE, HD), jnp.float32)
        for i in tiles:
            rows = slice(i * TILE, (i + 1) * TILE)
            ok = allowed(ids, mask, i, e - i)
            level = jnp.where(ok, totals[:, rows], jnp.float32(-NEG))
            scores = dot_nt(keys, q[rows]) * jnp.float32(SCALING * LOG2E)
            weight = jnp.exp2(scores - level)
            probs = dot_nt(values, g[rows])
            ds = (weight * (probs - deltas[:, rows])).astype(jnp.bfloat16)
            dsx[e * TILE : (e + 1) * TILE, rows] = ds
            dk = dk + dot_nn(ds, q[rows])
            dv = dv + dot_nn(weight.astype(jnp.bfloat16), g[rows])
        dk = dk * jnp.float32(SCALING)
        part = (e % 2) * TILE
        target = (dl, do, dr)[e // 2]
        target[part : part + TILE, lanes] = dk.astype(target.dtype)
        target[TOK + part : TOK + part + TILE, lanes] = dv.astype(target.dtype)
    wide = eye(TILE)
    for i in range(TILES_DEV):
        rows = slice(i * TILE, (i + 1) * TILE)
        window = slice(i * TILE, (i + WIN) * TILE)
        turned = dot_nn(kt[:, window], dsx[window, rows]) * jnp.float32(SCALING)
        dq[rows] = dot_nt(wide, turned.astype(jnp.bfloat16)).astype(jnp.bfloat16)


def attention_specs():
    narrow = pl.BlockSpec((TOK, HD), lambda h, *_: (0, h))
    whole = pl.BlockSpec(memory_space=pltpu.VMEM)
    return narrow, whole


def attention_forward(ids, mask, q, both, before, after):
    narrow, whole = attention_specs()
    return pl.pallas_call(
        forward_kernel,
        grid_spec=pltpu.PrefetchScalarGridSpec(
            num_scalar_prefetch=2,
            grid=(2,),
            in_specs=[whole] * 4,
            out_specs=[narrow, whole, whole],
            scratch_shapes=[pltpu.VMEM((3 * TOK, HD), jnp.bfloat16)] * 2,
        ),
        out_shape=[
            jax.ShapeDtypeStruct((TOK, 2 * HD), jnp.bfloat16),
            jax.ShapeDtypeStruct((TOK, 2 * HD), jnp.bfloat16),
            jax.ShapeDtypeStruct((2, 8, TOK), jnp.float32),
        ],
        cost_estimate=pl.CostEstimate(
            flops=700_000_000, bytes_accessed=2_400_000, transcendentals=1_300_000
        ),
        compiler_params=pltpu.CompilerParams(vmem_limit_bytes=VMEM_BYTES),
        name="attention_forward",
    )(ids, mask, q, both, before, after)


def attention_backward(ids, mask, q, both, before, after, g, att, stats):
    narrow, whole = attention_specs()
    return pl.pallas_call(
        backward_kernel,
        grid_spec=pltpu.PrefetchScalarGridSpec(
            num_scalar_prefetch=2,
            grid=(2,),
            in_specs=[whole] * 7,
            out_specs=[narrow, whole, whole, whole],
            scratch_shapes=[pltpu.VMEM((3 * TOK, HD), jnp.bfloat16)] * 2
            + [
                pltpu.VMEM((TOK, HD), jnp.bfloat16),
                pltpu.VMEM((TOK, HD), jnp.bfloat16),
                pltpu.VMEM((3 * TOK, TOK), jnp.bfloat16),
                pltpu.VMEM((HD, 3 * TOK), jnp.bfloat16),
            ],
        ),
        out_shape=[
            jax.ShapeDtypeStruct((TOK, 2 * HD), jnp.bfloat16),
            jax.ShapeDtypeStruct((2 * TOK, 2 * HD), jnp.bfloat16),
            jax.ShapeDtypeStruct((2 * TOK, 2 * HD), jnp.float32),
            jax.ShapeDtypeStruct((2 * TOK, 2 * HD), jnp.bfloat16),
        ],
        cost_estimate=pl.CostEstimate(
            flops=1_800_000_000, bytes_accessed=5_000_000, transcendentals=1_300_000
        ),
        compiler_params=pltpu.CompilerParams(vmem_limit_bytes=VMEM_BYTES),
        name="attention_backward",
    )(ids, mask, q, both, before, after, g, att, stats)


def pack_kernel(ids, w, o0, o1, o2, o3, buf, strips, sems):
    here = ids[2]
    far = ids[3]
    rows = pl.ds(pl.multiple_of(ids[1] * HD, HD), HD)
    copies = []
    for c in range(STRIPS):
        lanes = slice(c * STRIP, (c + 1) * STRIP)
        copies.append(pltpu.make_async_copy(w.at[rows, lanes], buf.at[:, lanes], sems.at[c]))
    for copy in copies:
        copy.start()
    for xhi in range(2):
        copies[2 * xhi].wait()
        copies[2 * xhi + 1].wait()
        for place, p in enumerate(ORDER):
            start = pl.multiple_of((xhi * 4 + (far ^ p)) * GROUP, GROUP)
            both = buf[:, pl.ds(start, GROUP)]
            for zp in range(2):
                strips[xhi * 2 + zp, :, place * CB : (place + 1) * CB] = both[
                    :, zp * CB : (zp + 1) * CB
                ]
    for p, out in enumerate((o0, o1, o2, o3)):
        out[...] = strips[here ^ p]


def pack_weights(ids, w):
    return pl.pallas_call(
        pack_kernel,
        in_specs=[pl.BlockSpec(memory_space=pltpu.SMEM), pl.BlockSpec(memory_space=pl.ANY)],
        out_specs=[pl.BlockSpec(memory_space=pltpu.VMEM)] * 4,
        scratch_shapes=[
            pltpu.VMEM((HD, D), jnp.bfloat16),
            pltpu.VMEM((4, HD, STRIP), jnp.bfloat16),
            pltpu.SemaphoreType.DMA((STRIPS,)),
        ],
        out_shape=[jax.ShapeDtypeStruct((HD, STRIP), jnp.bfloat16)] * 4,
        cost_estimate=pl.CostEstimate(flops=0, bytes_accessed=2_600_000, transcendentals=0),
        compiler_params=pltpu.CompilerParams(vmem_limit_bytes=VMEM_BYTES),
        name="pack_weights",
    )(ids, w)


def project_kernel(part, ids, *refs):
    mine, other, gathered, outs = refs[:4], refs[4:8], refs[8:12], refs[12:14]
    near, wide, flat = refs[14:]
    core = ids[1]
    lanes = slice(part * GROUP, (part + 1) * GROUP)
    for r in range(4):
        base = r * 2 * HD
        near[:, base : base + 2 * HD] = gathered[r][...]
        wide[pl.ds(pl.multiple_of(base + core * HD, HD), HD)] = mine[r][:, lanes]
        wide[pl.ds(pl.multiple_of(base + (1 - core) * HD, HD), HD)] = other[r][:, lanes]
    grown = dot_nn(near[...], wide[...]).astype(jnp.bfloat16)
    unit = eye(HD)
    for t in range(GROUP // HD):
        cols = slice(t * HD, (t + 1) * HD)
        flat[cols] = dot_nt(unit, grown[:, cols]).astype(jnp.bfloat16)
    for place, out in enumerate(outs):
        out[...] = flat[place * CB : (place + 1) * CB]


def project(ids, mine, other, gathered, part):
    whole = pl.BlockSpec(memory_space=pltpu.VMEM)
    return pl.pallas_call(
        functools.partial(project_kernel, part),
        in_specs=[pl.BlockSpec(memory_space=pltpu.SMEM)] + [whole] * 12,
        out_specs=[whole] * 2,
        scratch_shapes=[
            pltpu.VMEM((TOK, 8 * HD), jnp.bfloat16),
            pltpu.VMEM((8 * HD, GROUP), jnp.bfloat16),
            pltpu.VMEM((GROUP, TOK), jnp.bfloat16),
        ],
        out_shape=[jax.ShapeDtypeStruct((CB, TOK), jnp.bfloat16)] * 2,
        cost_estimate=pl.CostEstimate(
            flops=670_000_000, bytes_accessed=3_000_000, transcendentals=0
        ),
        compiler_params=pltpu.CompilerParams(vmem_limit_bytes=VMEM_BYTES),
        name="project",
    )(ids, *mine, *other, *gathered)


def weight_grad_kernel(ids, up, att, mine, other, buf, turned, sems):
    first_core = ids[1] == 0
    plane = ids[4]
    copies = [
        pltpu.make_async_copy(up.at[:, c * STRIP : (c + 1) * STRIP], buf.at[c], sems.at[c])
        for c in range(STRIPS)
    ]
    for copy in copies:
        copy.start()
    turned[...] = dot_nt(eye(2 * HD), att[...]).astype(jnp.bfloat16)
    for c, copy in enumerate(copies):
        copy.wait()
        halves = [
            dot_nn(turned[...], buf[c, :, base : base + GROUP]).astype(jnp.bfloat16)
            for base in (0, GROUP)
        ]
        lanes = pl.ds(pl.multiple_of((c ^ (plane // 2)) * GROUP, GROUP), GROUP)
        for target, low in ((mine, first_core), (other, jnp.logical_not(first_core))):
            first, second = (jnp.where(low, x[:, 0:CB], x[:, CB:GROUP]) for x in halves)
            straight = (plane & 1) == 0
            target[:, lanes] = jnp.concatenate(
                [jnp.where(straight, first, second), jnp.where(straight, second, first)], axis=1
            )


def weight_grad(ids, up, att):
    whole = pl.BlockSpec(memory_space=pltpu.VMEM)
    return pl.pallas_call(
        weight_grad_kernel,
        in_specs=[
            pl.BlockSpec(memory_space=pltpu.SMEM),
            pl.BlockSpec(memory_space=pl.ANY),
            whole,
        ],
        out_specs=[whole, whole],
        scratch_shapes=[
            pltpu.VMEM((STRIPS, TOK, STRIP), jnp.bfloat16),
            pltpu.VMEM((2 * HD, TOK), jnp.bfloat16),
            pltpu.SemaphoreType.DMA((STRIPS,)),
        ],
        out_shape=[jax.ShapeDtypeStruct((2 * HD, PLANE * CB), jnp.bfloat16)] * 2,
        cost_estimate=pl.CostEstimate(
            flops=1_700_000_000, bytes_accessed=8_000_000, transcendentals=0
        ),
        compiler_params=pltpu.CompilerParams(vmem_limit_bytes=VMEM_BYTES),
        name="weight_grad",
    )(ids, up, att)


def merge_kernel(mine, near, keep, send):
    for target, lanes in ((keep, slice(0, STRIP)), (send, slice(STRIP, 2 * STRIP))):
        total = mine[:, lanes].astype(jnp.float32) + near[:, lanes].astype(jnp.float32)
        target[...] = total.astype(jnp.bfloat16)


def merge(mine, near):
    whole = pl.BlockSpec(memory_space=pltpu.VMEM)
    return pl.pallas_call(
        merge_kernel,
        in_specs=[whole] * 2,
        out_specs=[whole] * 2,
        out_shape=[jax.ShapeDtypeStruct((2 * HD, STRIP), jnp.bfloat16)] * 2,
        cost_estimate=pl.CostEstimate(
            flops=1_000_000, bytes_accessed=4_000_000, transcendentals=0
        ),
        compiler_params=pltpu.CompilerParams(vmem_limit_bytes=VMEM_BYTES),
        name="merge",
    )(mine, near)


def merge_planes_kernel(keep, came, *outs):
    for p, out in enumerate(outs):
        lanes = slice(p * CB, (p + 1) * CB)
        total = keep[:, lanes].astype(jnp.float32) + came[:, lanes].astype(jnp.float32)
        out[...] = total.astype(jnp.bfloat16)


def merge_planes(keep, came):
    whole = pl.BlockSpec(memory_space=pltpu.VMEM)
    return pl.pallas_call(
        merge_planes_kernel,
        in_specs=[whole] * 2,
        out_specs=[whole] * 4,
        out_shape=[jax.ShapeDtypeStruct((2 * HD, CB), jnp.bfloat16)] * 4,
        cost_estimate=pl.CostEstimate(
            flops=1_000_000, bytes_accessed=2_000_000, transcendentals=0
        ),
        compiler_params=pltpu.CompilerParams(vmem_limit_bytes=VMEM_BYTES),
        name="merge_planes",
    )(keep, came)


def gram_kernel(*refs):
    parts, (left, right) = refs[:4], refs[4:]
    highest = lax.Precision.HIGHEST
    total = parts[0][...].astype(jnp.float32)
    for part in parts[1:]:
        total = total + part[...].astype(jnp.float32)
    for h in range(2):
        block = total[h * HD : (h + 1) * HD]
        squares = jnp.sum(block * block, axis=0, keepdims=True)
        trace = jnp.sum(squares, axis=1, keepdims=True)
        inverse = 1.0 / (trace + epsilon)
        turned = block.T
        left[h, 0] = dot_nt(block, block, highest) * (inverse * HD)
        right[h, 0] = dot_nt(turned, turned, highest) * (inverse * CB)


def gram(parts):
    whole = pl.BlockSpec(memory_space=pltpu.VMEM)
    return pl.pallas_call(
        gram_kernel,
        in_specs=[whole] * 4,
        out_specs=[whole] * 2,
        out_shape=[
            jax.ShapeDtypeStruct((2, 1, HD, HD), jnp.float32),
            jax.ShapeDtypeStruct((2, 1, CB, CB), jnp.float32),
        ],
        cost_estimate=pl.CostEstimate(
            flops=400_000_000, bytes_accessed=2_000_000, transcendentals=0
        ),
        compiler_params=pltpu.CompilerParams(vmem_limit_bytes=VMEM_BYTES),
        name="gram",
    )(*parts)


def settle_kernel(own, first, second, dk, dv):
    total = own[...] + first[...].astype(jnp.float32) + second[...].astype(jnp.float32)
    dk[...] = total[0:TOK].astype(jnp.bfloat16)
    dv[...] = total[TOK : 2 * TOK].astype(jnp.bfloat16)


def settle(own, first, second):
    whole = pl.BlockSpec(memory_space=pltpu.VMEM)
    return pl.pallas_call(
        settle_kernel,
        in_specs=[whole] * 3,
        out_specs=[whole] * 2,
        out_shape=[jax.ShapeDtypeStruct((TOK, 2 * HD), jnp.bfloat16)] * 2,
        cost_estimate=pl.CostEstimate(
            flops=1_000_000, bytes_accessed=3_000_000, transcendentals=0
        ),
        compiler_params=pltpu.CompilerParams(vmem_limit_bytes=VMEM_BYTES),
        name="settle",
    )(own, first, second)


def pair_kernel(q, k, v, queries, both, sems):
    copies = [
        pltpu.make_async_copy(k, both.at[:, 0 : 2 * HD], sems.at[0]),
        pltpu.make_async_copy(v, both.at[:, 2 * HD : 4 * HD], sems.at[1]),
        pltpu.make_async_copy(q, queries, sems.at[2]),
    ]
    for copy in copies:
        copy.start()
    for copy in copies:
        copy.wait()


def pair_up(q, k, v):
    return pl.pallas_call(
        pair_kernel,
        in_specs=[pl.BlockSpec(memory_space=pl.ANY)] * 3,
        out_specs=[pl.BlockSpec(memory_space=pltpu.VMEM)] * 2,
        scratch_shapes=[pltpu.SemaphoreType.DMA((3,))],
        out_shape=[
            jax.ShapeDtypeStruct((TOK, 2 * HD), jnp.bfloat16),
            jax.ShapeDtypeStruct((TOK, 4 * HD), jnp.bfloat16),
        ],
        cost_estimate=pl.CostEstimate(flops=0, bytes_accessed=1_500_000, transcendentals=0),
        compiler_params=pltpu.CompilerParams(vmem_limit_bytes=VMEM_BYTES),
        name="pair_up",
    )(q, k, v)


def in_hbm(x):
    return pltpu.with_memory_space_constraint(x, pltpu.HBM)


def local(query_states, key_states, value_states, out_weight, upstream, tile_mask):
    frame = lax.axis_index(FRAME).astype(jnp.int32)
    core = lax.axis_index("core").astype(jnp.int32)
    here = lax.axis_index(NEAR).astype(jnp.int32)
    far = lax.axis_index("zq").astype(jnp.int32)
    plane = lax.axis_index(("xlo", "y")).astype(jnp.int32)
    ids = jnp.stack([frame, core, here, far, plane])
    frames = lax.axis_size(FRAME)
    up = [(i, i + 1) for i in range(frames - 1)]
    down = [(j, i) for i, j in up]
    cores = [(0, 1), (1, 0)]
    mask = tile_mask.T
    query_states = in_hbm(query_states)
    key_states = in_hbm(key_states)
    value_states = in_hbm(value_states)

    queries, both = pair_up(query_states, key_states, value_states)
    before = lax.ppermute(both, FRAME, up)
    after = lax.ppermute(both, FRAME, down)

    grad_attended = lax.dot_general(
        upstream, out_weight, (((1,), (1,)), ((), ())), preferred_element_type=jnp.float32
    ).astype(jnp.bfloat16)
    strips_mine = list(pack_weights(ids, in_hbm(out_weight)))
    for p in (3, 2, 1):
        pairs = [(i, i ^ p) for i in range(4)]
        strips_mine[p] = lax.ppermute(strips_mine[p], NEAR, pairs)
    strips_other = []
    for p in range(4):
        strips_other.append(lax.ppermute(strips_mine[p], "core", cores))

    attended, att, stats = attention_forward(ids, mask, queries, both, before, after)
    gathered = [att] * 4
    for p in (3, 2, 1):
        pairs = [(i, i ^ p) for i in range(4)]
        gathered[p] = lax.ppermute(att, NEAR, pairs)

    half_mine, half_other = weight_grad(ids, in_hbm(upstream), att)
    half_near = lax.ppermute(half_other, "core", cores)
    keep, send = merge(half_mine, half_near)
    came = lax.ppermute(send, "xlo", cores)
    quarters = merge_planes(keep, came)
    grad_parts = [quarters[0]]
    for p in (2, 3, 1):
        pairs = [(i, i ^ p) for i in range(4)]
        grad_parts.append(lax.ppermute(quarters[p], "y", pairs))

    partials = []
    arrived = []
    for place, p in enumerate(ORDER):
        if place % 2 == 0:
            partials += project(ids, strips_mine, strips_other, gathered, place // 2)
        if p:
            pairs = [(i, i ^ p) for i in range(4)]
            arrived.append(lax.ppermute(partials[place], "zq", pairs))
    projected = partials[3].astype(jnp.float32)
    for partial in arrived:
        projected = projected + partial.astype(jnp.float32)
    projected = projected.astype(jnp.bfloat16).T

    grad_query, left, own, right = attention_backward(
        ids,
        mask,
        queries,
        both,
        before,
        after,
        grad_attended,
        att,
        stats,
    )
    from_right = lax.ppermute(left, FRAME, down)
    from_left = lax.ppermute(right, FRAME, up)
    grad_key, grad_value = settle(own, from_right, from_left)

    gram_left, gram_right = gram(grad_parts)
    return (attended, projected, grad_query, grad_key, grad_value, gram_left, gram_right)


def solution(mesh):
    fine = Mesh(mesh.devices.reshape(2, 4, 2, 2, 4, 2), FRAME + HEAD)
    placed = (
        P(FRAME, HEAD),
        P(FRAME, HEAD),
        P(FRAME, HEAD),
        P(HEAD, None),
        P(FRAME, None),
        P(),
    )
    return jax.shard_map(
        local,
        mesh=fine,
        in_specs=placed,
        out_specs=(
            P(FRAME, HEAD),
            P(FRAME, HEAD),
            P(FRAME, HEAD),
            P(FRAME, HEAD),
            P(FRAME, HEAD),
            P(HEAD, FRAME, None, None),
            P(HEAD, FRAME, None, None),
        ),
        check_vma=False,
    )
```
